256 devices in a mesh: tile: 32 (over y_hi, z, core), slide: 8 (over x, y_lo).
Axes of the slice: x: 4, y: 4 (y_hi: 2, y_lo: 2; y = y_hi * 2 + y_lo), z: 8, core: 2. Of those that a mesh axis runs over, the one named last changes fastest.
Arguments:
- tokens: bfloat16 [768, 64, 384], P(('slide', 'tile')), parts along dimension 0, may hold values from -6 to 6
- tissue: int32 [768, 64], P(('slide', 'tile')), parts along dimension 0, may hold values from 0 to 1, as said below
- dw_kernel: bfloat16 [7, 7, 384], replicated, may hold values from -0.875 to 0.875
- w_fc1: bfloat16 [384, 1536], replicated, may hold values from -0.3125 to 0.3125
- w_fc2: bfloat16 [1536, 384], replicated, may hold values from -0.15625 to 0.15625
- layer_scale: float32 [384], replicated, may hold values from 0.3 to 3
- w_query: bfloat16 [384, 1024], replicated, may hold values from -16 to 16
- w_key: bfloat16 [384, 1024], replicated, may hold values from -0.3125 to 0.3125
- w_value: bfloat16 [384, 1024], replicated, may hold values from -0.3125 to 0.3125
- w_out: bfloat16 [1024, 384], replicated, may hold values from -0.1875 to 0.1875
Outputs:
- encoded: bfloat16 [768, 64, 384], P(('slide', 'tile')), parts along dimension 0
The draws below stay inside these ranges and needn't reach their ends.
There are 8 independent parts, one for each index of `slide`. The reference program is written for one: setup_inputs(seed, part) draws one part's arguments, and reference() takes and returns one part's arrays. A program takes and returns all parts, laid end to end along the dimension named above; an argument that names none is the same for every part. Nothing has to cross between parts.
Inputs may be any that keep to these rules, and one draw needn't show every extreme that they name: Among the 192 tiles of each aligned block of 3 grid rows at most 96 hold tissue, and at least one; some block holds exactly 96.
All inputs are finite; a program needn't handle non-finite values.
Results may differ from the reference program's by a relative error of at most 0.035.
Values may be sent and summed in bfloat16 or wider, within the bound.
A program may use at most 192 MiB of HBM per device.

```python
import math
import jax
import jax.numpy as jnp
from jax import lax

C = 384
HID = 1536
HEADS = 16
HD = 64
GW = 64
ROWS_DEV = 3
TOK_DEV = 192
ROWS = 96
CAP = 96
N_TILE = 32


def draw_tissue(key, part):
    blocks = ROWS // ROWS_DEV
    key_count, key_full, key_perm = jax.random.split(jax.random.fold_in(key, 11), 3)
    counts = jax.random.randint(key_count, (blocks,), max(1, CAP // 8), CAP + 1)
    fullest = jax.random.randint(key_full, (), 0, blocks)
    counts = jnp.where(jnp.arange(blocks) == fullest, CAP, counts)
    perm_keys = jax.random.split(key_perm, blocks)
    ranks = jax.vmap(lambda single: jax.random.permutation(single, TOK_DEV))(perm_keys)
    mask = (ranks < counts[:, None]).astype(jnp.int32)
    return mask.reshape(ROWS, GW)


def draw_w_query(key, part):
    key_base = jax.random.fold_in(jax.random.fold_in(key, 23), 0)
    base = jax.random.normal(key_base, (C, HEADS * HD), jnp.float32) * C ** (-0.5)
    base = jnp.clip(base, -16.0, 16.0)
    return base.astype(jnp.bfloat16)


def level_of(rng, extent, pieces, low, largest):
    def one(dim, parts):
        steps = jax.random.uniform(jax.random.fold_in(jax.random.fold_in(rng, 6), dim), (parts,), jnp.float32, low / len(pieces), largest / len(pieces))
        return jnp.repeat(jnp.exp(steps), extent[dim] // parts).reshape((-1,) + (1,) * (len(extent) - dim - 1))

    gain = one(*pieces[0])
    for cut in pieces[1:]:
        gain = gain * one(*cut)
    return gain


def bell_draw(rng, dims, scale, limit, cuts=(), kind=jnp.bfloat16):
    loudness = level_of(rng, dims, cuts, -0.22, 0.18) if cuts else 1.0
    drawn = jax.random.normal(rng, dims, jnp.float32) * scale * loudness
    return jnp.minimum(jnp.maximum(drawn, -limit), limit).astype(kind)


def setup_inputs(seed: int = 0, part: int = 0) -> dict:
    keys = jax.random.split(jax.random.key(seed), 11)
    part_keys = jax.random.split(jax.random.fold_in(keys[10], part), 11)
    tokens = bell_draw(part_keys[0], (ROWS, GW, C), 1.0, 6.0, ((0, 32),))
    tissue = draw_tissue(jax.random.fold_in(jax.random.fold_in(keys[10], part), 71), part)
    dw_kernel = bell_draw(keys[2], (7, 7, C), 49 ** -0.5, 0.875)
    w_fc1 = bell_draw(keys[3], (C, HID), C ** -0.5, 0.3125)
    w_fc2 = bell_draw(keys[4], (HID, C), HID ** -0.5, 0.15625)
    layer_scale = jnp.clip(jnp.exp(jax.random.uniform(keys[5], (C,), jnp.float32, math.log(0.3), math.log(3.0))), 0.3, 3.0)
    w_query = draw_w_query(jax.random.fold_in(keys[10], 71), part)
    w_key = bell_draw(keys[7], (C, HEADS * HD), C ** -0.5, 0.3125)
    w_value = bell_draw(keys[8], (C, HEADS * HD), C ** -0.5, 0.3125)
    w_out = bell_draw(keys[9], (HEADS * HD, C), (HEADS * HD) ** -0.5, 0.1875)
    return dict(tokens=tokens, tissue=tissue, dw_kernel=dw_kernel, w_fc1=w_fc1, w_fc2=w_fc2, layer_scale=layer_scale, w_query=w_query, w_key=w_key, w_value=w_value, w_out=w_out)


def layer_norm(x):
    mean = lax.optimization_barrier(jnp.mean(x, axis=-1, keepdims=True))
    centred = x - mean
    var = lax.optimization_barrier(jnp.mean(centred * centred, axis=-1, keepdims=True))
    return centred * lax.rsqrt(var + 1e-06)

def reference(tokens, tissue, dw_kernel, w_fc1, w_fc2, layer_scale, w_query, w_key, w_value, w_out):
    masked = tokens * tissue[:, :, None].astype(jnp.bfloat16)
    nrows, width, chans = masked.shape
    padded = jnp.pad(masked.astype(jnp.float32), ((3, 3), (3, 3), (0, 0)))
    kernel = dw_kernel.astype(jnp.float32)
    conv = jnp.zeros((nrows, width, chans), jnp.float32)
    for offs_i in range(7):
        for offs_j in range(7):
            conv = conv + padded[offs_i:offs_i + nrows, offs_j:offs_j + width] * kernel[offs_i, offs_j]
    flat_masked = masked.reshape(nrows * width, chans)
    normed1 = layer_norm(conv.reshape(nrows * width, chans)).astype(jnp.bfloat16)
    hidden = jax.nn.gelu(jnp.dot(normed1, w_fc1, preferred_element_type=jnp.float32), approximate=False).astype(jnp.bfloat16)
    branch = jnp.dot(hidden, w_fc2, preferred_element_type=jnp.float32)
    section = (flat_masked.astype(jnp.float32) + layer_scale * branch).astype(jnp.bfloat16)
    normed2 = layer_norm(section.astype(jnp.float32)).astype(jnp.bfloat16)
    query = jnp.dot(normed2, w_query, preferred_element_type=jnp.float32).astype(jnp.bfloat16)
    key = jnp.dot(normed2, w_key, preferred_element_type=jnp.float32).astype(jnp.bfloat16)
    value = jnp.dot(normed2, w_value, preferred_element_type=jnp.float32).astype(jnp.bfloat16)
    ntok = nrows * width
    key_heads = key.reshape(ntok, HEADS, HD).astype(jnp.float32)
    value_heads = value.reshape(ntok, HEADS, HD).astype(jnp.float32)
    flags = tissue.reshape(ntok) > 0
    query_blocks = query.reshape(N_TILE, ntok // N_TILE, HEADS, HD)

    def per_block(qblock):
        scores = jnp.einsum('qhd,khd->hqk', qblock.astype(jnp.float32), key_heads) * 0.125
        scores = jnp.where(flags[None, None, :], scores, -1e+30)
        rowmax = lax.optimization_barrier(jnp.max(scores, axis=-1, keepdims=True))
        weights = jnp.where(flags[None, None, :], jnp.exp(scores - rowmax), 0.0)
        total = lax.optimization_barrier(jnp.sum(weights, axis=-1))
        probs = weights.astype(jnp.bfloat16).astype(jnp.float32)
        summed = jnp.einsum('hqk,khd->qhd', probs, value_heads)
        return (summed / jnp.transpose(total)[:, :, None]).astype(jnp.bfloat16)
    attended = lax.map(per_block, query_blocks).reshape(ntok, HEADS * HD)
    result = section.astype(jnp.float32) + jnp.dot(attended, w_out, preferred_element_type=jnp.float32)
    return result.astype(jnp.bfloat16).reshape(nrows, width, chans)
```

```python
import functools

import jax
import jax.numpy as jnp
from jax import lax
from jax.experimental import pallas as pl
from jax.experimental.pallas import tpu as pltpu
from jax.sharding import PartitionSpec as P

HEADS = 16
HD = 64
CAP = 96
ROWS = 3
GW = 64
C = 384
HID = 1536
TOK = ROWS * GW
UNIT = 2 * CAP
CHUNK = 4 * CAP
NCHUNK = 8
KS = 2 * CHUNK
QUADS = 4
QW = 256
MARK = 1024.0
NEG = -1e30

f32 = jnp.float32
bf16 = jnp.bfloat16
LAST = (((1,), (1,)), ((), ()))


def layer_norm(x):
    mean = jnp.mean(x, axis=-1, keepdims=True)
    centred = x - mean
    var = jnp.mean(centred * centred, axis=-1, keepdims=True)
    return centred * lax.rsqrt(var + 1e-06)


def matmul(a, b):
    return jnp.dot(a, b, preferred_element_type=f32)


def kernel(
    tokens, tissue, dw, w1, w2, scale, wq, wk, wv, wo, out,
    tok, tis, dwv, dwf, w1v, w2v, scv, wqv, wkv, wvv, wov,
    halo, thalo, ext, conv, sec, xbuf, k_all, v_all, qblk,
    s_ref, p_ref, m_ref, l_ref, a_ref, acc,
    load_sem, misc_s, misc_r, ring_s, ring_r, par_s, par_r,
):
    me = lax.axis_index("tile")
    core = lax.rem(me, 2)
    z = lax.rem(lax.div(me, 2), 8)
    y = lax.div(me, 16)
    partner = me + 1 - 2 * core
    zup = y * 16 + lax.rem(z + 1, 8) * 2 + core
    zdn = y * 16 + lax.rem(z + 7, 8) * 2 + core
    yoth = (1 - y) * 16 + z * 2 + core
    upper = lax.rem(me + 1, 32)
    lower = lax.rem(me + 31, 32)
    beyond = lower + core * (upper - lower)
    nxt = zup + core * (zdn - zup)
    half = pl.ds(pl.multiple_of(core * UNIT, UNIT), UNIT)

    pairs = [(tokens, tok), (tissue, tis), (dw, dwv), (w1, w1v), (w2, w2v), (scale, scv),
             (wq, wqv), (wk, wkv), (wv, wvv), (wo, wov)]
    loads = [pltpu.make_async_copy(a, b, load_sem.at[i]) for i, (a, b) in enumerate(pairs)]
    for load in loads:
        load.start()

    barrier = pltpu.get_barrier_semaphore()
    for other in (partner, zup, zdn, yoth, beyond):
        pl.semaphore_signal(barrier, inc=1, device_id={"tile": other},
                            device_id_type=pl.DeviceIdType.MESH)
    pl.semaphore_wait(barrier, 5)

    def remote(src, dst, send, recv, device):
        return pltpu.make_async_remote_copy(
            src_ref=src, dst_ref=dst, send_sem=send, recv_sem=recv,
            device_id={"tile": device}, device_id_type=pl.DeviceIdType.MESH)

    def misc(src, dst, i, device):
        return remote(src, dst, misc_s.at[i], misc_r.at[i], device)

    halos = [
        misc(tokens, halo.at[0], 0, upper), misc(tokens, halo.at[1], 1, lower),
        misc(tissue, thalo.at[0], 2, upper), misc(tissue, thalo.at[1], 3, lower),
    ]
    for copy in halos:
        copy.start()

    eye = lax.broadcasted_iota(jnp.int32, (GW, GW), 0) == lax.broadcasted_iota(jnp.int32, (GW, GW), 1)

    def column(row):
        return jnp.sum(jnp.where(eye, row.astype(f32), 0.0), axis=1, keepdims=True)

    col_ids = lax.broadcasted_iota(jnp.int32, (GW, 128), 0)

    def conv_pass(rows, first):
        @pl.loop(0, C // 128)
        def _(tile):
            lanes = pl.ds(pl.multiple_of(tile * 128, 128), 128)
            for r in range(ROWS):
                total = None
                for j in range(7):
                    part = None
                    for i in range(7):
                        if r + i in rows:
                            term = ext[r + i, :, lanes] * dwf[i, pl.ds(j, 1), lanes]
                            part = term if part is None else part + term
                    if part is None:
                        continue
                    s = j - 3
                    if s:
                        moved = pltpu.roll(part, (-s) % GW, 0)
                        inside = (col_ids + s >= 0) & (col_ids + s < GW)
                        part = jnp.where(inside, moved, 0.0)
                    total = part if total is None else total + part
                where = pl.ds(r * GW, GW)
                conv[where, lanes] = total if first else conv[where, lanes] + total

    for i in range(3):
        loads[i].wait()
    dwf[...] = dwv[...].astype(f32)
    for r in range(ROWS):
        ext[3 + r] = tok[r].astype(f32) * column(tis[r : r + 1, :])
    conv_pass((3, 4, 5), True)
    for copy in halos:
        copy.wait_recv()
    has_low = jnp.where(me > 0, 1.0, 0.0)
    has_high = jnp.where(me < 31, 1.0, 0.0)
    for r in range(ROWS):
        ext[r] = halo[0, r].astype(f32) * (column(thalo[0, r : r + 1, :]) * has_low)
        ext[6 + r] = halo[1, r].astype(f32) * (column(thalo[1, r : r + 1, :]) * has_high)
    conv_pass((0, 1, 2, 6, 7, 8), False)

    normed1 = layer_norm(conv[...]).astype(bf16)
    for i in range(3, 6):
        loads[i].wait()
    branch = None
    for n in range(3):
        cut = slice(n * 512, (n + 1) * 512)
        h = matmul(normed1, w1v[:, cut])
        h = (0.5 * h * (1.0 + lax.erf(h * 0.7071067811865476))).astype(bf16)
        part = matmul(h, w2v[cut, :])
        branch = part if branch is None else branch + part
    masked = ext[3:6].reshape(TOK, C)
    section = (masked + scv[...][None, :] * branch).astype(bf16)
    sec[...] = section
    normed2 = layer_norm(section.astype(f32)).astype(bf16)

    flags = tis[...].astype(f32)
    before = lax.broadcasted_iota(jnp.int32, (GW, GW), 0) < lax.broadcasted_iota(jnp.int32, (GW, GW), 1)
    rank = matmul(flags.astype(bf16), jnp.where(before, 1.0, 0.0).astype(bf16))
    counts = jnp.sum(flags, axis=1, keepdims=True)
    slot = lax.broadcasted_iota(jnp.int32, (CAP, GW), 0).astype(f32)
    x = jnp.zeros((CAP, C), f32)
    offset = jnp.zeros((1, 1), f32)
    for r in range(ROWS):
        pick = (slot == rank[r : r + 1, :] + offset) & (flags[r : r + 1, :] > 0)
        x = x + matmul(jnp.where(pick, 1.0, 0.0).astype(bf16), normed2[r * GW : (r + 1) * GW, :])
        offset = offset + counts[r : r + 1, :]
    empty = (lax.broadcasted_iota(jnp.int32, (CAP, C), 0).astype(f32) >= offset) & (
        lax.broadcasted_iota(jnp.int32, (CAP, C), 1) == 0)
    x = jnp.where(empty, MARK, x).astype(bf16)

    own = xbuf.at[0, pl.ds(pl.multiple_of(core * CAP, CAP), CAP)]
    far = xbuf.at[0, pl.ds(pl.multiple_of(UNIT + core * CAP, CAP), CAP)]
    xbuf[0, pl.ds(pl.multiple_of(core * CAP, CAP), CAP), :] = x
    own_copy = misc(own, own, 4, partner)
    far_copy = misc(own, far, 5, yoth)
    far_share = misc(far, far, 6, partner)
    own_copy.start()
    far_copy.start()

    def ring(src, dst):
        return remote(xbuf.at[src, half], xbuf.at[dst, half], ring_s.at[dst], ring_r.at[dst], nxt)

    def share(c):
        return remote(xbuf.at[c, half], xbuf.at[c, half], par_s.at[c], par_r.at[c], partner)

    def first_ring(unit, dst):
        return remote(xbuf.at[0, pl.ds(unit * UNIT, UNIT)], xbuf.at[dst, half],
                      ring_s.at[dst], ring_r.at[dst], nxt)

    own_copy.wait_recv()
    first_ring(0, 1).start()

    loads[6].wait()
    lane = lax.broadcasted_iota(jnp.int32, (TOK, QW), 1)
    for g in range(QUADS):
        query = matmul(normed2, wqv[:, g * QW : (g + 1) * QW]).astype(bf16).astype(f32) * 0.125
        for h in range(4):
            mine = (lane >= h * HD) & (lane < (h + 1) * HD)
            qblk[g, h * TOK : (h + 1) * TOK, :] = jnp.where(mine, query, 0.0).astype(bf16)
    m_ref[...] = jnp.full(m_ref.shape, NEG, f32)
    l_ref[...] = jnp.zeros(l_ref.shape, f32)
    acc[...] = jnp.zeros(acc.shape, f32)

    far_copy.wait_recv()
    far_share.start()
    far_share.wait_recv()
    first_ring(1, 2).start()
    loads[7].wait()
    loads[8].wait()

    first_lane = jnp.where(lax.broadcasted_iota(jnp.int32, (8, C), 1) == 0, 1.0, 0.0).astype(bf16)

    def project(c):
        rows = pl.ds(pl.multiple_of(c * CHUNK, CHUNK), CHUNK)
        xc = xbuf[c]
        for n in range(4):
            cut = slice(n * 256, (n + 1) * 256)
            k_all[rows, cut] = matmul(xc, wkv[:, cut]).astype(bf16)
            v_all[rows, cut] = matmul(xc, wvv[:, cut]).astype(bf16)

    project(0)
    ring(0, 1).wait_recv()
    ring(1, 3).start()
    share(1).start()
    share(1).wait_recv()
    project(1)

    half_lane = lax.broadcasted_iota(jnp.int32, (TOK, 128), 1) < HD

    def scores(p, g):
        rows = pl.ds(pl.multiple_of(p * KS, KS), KS)
        s_ref[g % 2] = lax.dot_general(
            qblk[g], k_all[rows, g * QW : (g + 1) * QW], LAST, preferred_element_type=f32)

    def attend(p, g, shift):
        at = g % 2
        tiles = range(KS // 128)
        for r in range(0, 4 * TOK, 32):
            rs = slice(r, r + 32)
            st = [
                (s_ref[at, rs, t * 128 : (t + 1) * 128].reshape(4, 8, 128)
                 + shift[:, t * 128 : (t + 1) * 128][None]).reshape(32, 128)
                for t in tiles
            ]
            top = functools.reduce(jnp.maximum, st)
            old = m_ref[g, rs, :]
            new = jnp.maximum(old, jnp.max(top, axis=1, keepdims=True))
            factor = jnp.exp(old - new)
            m_ref[g, rs, :] = new
            a_ref[at, rs, :] = factor
            total = None
            for t in tiles:
                weight = jnp.exp(st[t] - new)
                p_ref[at, rs, t * 128 : (t + 1) * 128] = weight.astype(bf16)
                total = weight if total is None else total + weight
            l_ref[g, rs, :] = l_ref[g, rs, :] * factor + total
        rows = pl.ds(pl.multiple_of(p * KS, KS), KS)
        o = matmul(p_ref[at], v_all[rows, g * QW : (g + 1) * QW])
        for t in range(2):
            a, b = slice(2 * t * TOK, (2 * t + 1) * TOK), slice((2 * t + 1) * TOK, (2 * t + 2) * TOK)
            cut = slice(t * 128, (t + 1) * 128)
            o_t = jnp.where(half_lane, o[a, cut], o[b, cut])
            f_t = jnp.where(half_lane, a_ref[at, a, :], a_ref[at, b, :])
            dst = slice(g * QW + t * 128, g * QW + (t + 1) * 128)
            acc[:, dst] = acc[:, dst] * f_t + o_t

    @pl.loop(0, 4)
    def _(p):
        even, odd = 2 * p + 2, 2 * p + 3
        marks = [
            lax.dot_general(first_lane, xbuf[2 * p + i], LAST, preferred_element_type=f32) for i in range(2)
        ]
        shift = jnp.where(jnp.concatenate(marks, axis=1) > 0.5 * MARK, NEG, 0.0)
        scores(p, 0)
        attend(p, 0, shift)

        @pl.when(p < 3)
        def _():
            ring(even, even).wait_recv()
            share(even).start()

        @pl.when(p < 2)
        def _():
            ring(even, even + 2).start()

        @pl.when(p == 2)
        def _():
            ring(5 + core, 7).start()

        scores(p, 1)
        attend(p, 1, shift)

        @pl.when(p < 3)
        def _():
            ring(odd, odd).wait_recv()
            share(odd).start()

        @pl.when(p == 0)
        def _():
            ring(odd, odd + 2).start()

        @pl.when(p < 3)
        def _():
            share(even).wait_recv()
            project(even)

        scores(p, 2)
        attend(p, 2, shift)

        @pl.when(p < 3)
        def _():
            share(odd).wait_recv()
            project(odd)

        scores(p, 3)
        attend(p, 3, shift)

    loads[9].wait()
    result = sec[...].astype(f32)
    for g in range(QUADS):
        parts = []
        for t in range(2):
            a, b = slice(2 * t * TOK, (2 * t + 1) * TOK), slice((2 * t + 1) * TOK, (2 * t + 2) * TOK)
            total_a = jnp.sum(l_ref[g, a, :], axis=1, keepdims=True)
            total_b = jnp.sum(l_ref[g, b, :], axis=1, keepdims=True)
            dst = slice(g * QW + t * 128, g * QW + (t + 1) * 128)
            parts.append((acc[:, dst] / jnp.where(half_lane, total_a, total_b)).astype(bf16))
        result = result + matmul(jnp.concatenate(parts, axis=1), wov[g * QW : (g + 1) * QW, :])
    out[...] = result.astype(bf16).reshape(ROWS, GW, C)

    for copy in halos + [own_copy, far_copy, far_share]:
        copy.wait_send()
    for c in range(1, NCHUNK):
        ring(c, c).wait_send()
        share(c).wait_send()


def local(tokens, tissue, dw_kernel, w_fc1, w_fc2, layer_scale, w_query, w_key, w_value, w_out):
    vmem, sem = pltpu.VMEM, pltpu.SemaphoreType.DMA
    return pl.pallas_call(
        kernel,
        out_shape=jax.ShapeDtypeStruct((ROWS, GW, C), bf16),
        in_specs=[pl.BlockSpec(memory_space=pl.ANY)] * 10,
        out_specs=pl.BlockSpec(memory_space=pltpu.VMEM),
        scratch_shapes=[
            vmem((ROWS, GW, C), bf16), vmem((ROWS, GW), jnp.int32),
            vmem((7, 7, C), bf16), vmem((7, 7, C), f32),
            vmem((C, HID), bf16), vmem((HID, C), bf16), vmem((C,), f32),
            vmem((C, 1024), bf16), vmem((C, 1024), bf16), vmem((C, 1024), bf16), vmem((1024, C), bf16),
            vmem((2, ROWS, GW, C), bf16), vmem((2, ROWS, GW), jnp.int32),
            vmem((9, GW, C), f32), vmem((TOK, C), f32), vmem((TOK, C), bf16),
            vmem((NCHUNK, CHUNK, C), bf16),
            vmem((NCHUNK * CHUNK, 1024), bf16), vmem((NCHUNK * CHUNK, 1024), bf16),
            vmem((QUADS, 4 * TOK, QW), bf16),
            vmem((2, 4 * TOK, KS), f32), vmem((2, 4 * TOK, KS), bf16),
            vmem((QUADS, 4 * TOK, 128), f32), vmem((QUADS, 4 * TOK, 128), f32),
            vmem((2, 4 * TOK, 128), f32), vmem((TOK, 1024), f32),
            sem((10,)), sem((7,)), sem((7,)), sem((NCHUNK,)), sem((NCHUNK,)), sem((NCHUNK,)), sem((NCHUNK,)),
        ],
        compiler_params=pltpu.CompilerParams(
            collective_id=0, has_side_effects=True, vmem_limit_bytes=60 << 20),
        name="block",
    )(tokens, tissue, dw_kernel, w_fc1, w_fc2, layer_scale, w_query, w_key, w_value, w_out)


def solution(mesh):
    spec = P(("slide", "tile"), None, None)
    in_specs = (spec, P(("slide", "tile"), None)) + (P(),) * 8
    return jax.shard_map(local, mesh=mesh, in_specs=in_specs, out_specs=spec, check_vma=False)
```

```python
import functools

import jax
import jax.numpy as jnp
from jax import lax
from jax.experimental import pallas as pl
from jax.experimental.pallas import tpu as pltpu
from jax.sharding import PartitionSpec as P

HEADS = 16
HD = 64
CAP = 96
ROWS = 3
GW = 64
C = 384
HID = 1536
TOK = ROWS * GW
UNIT = 2 * CAP
CHUNK = 4 * CAP
NCHUNK = 8
KS = 2 * CHUNK
QUADS = 4
QW = 256
MARK = 1024.0
NEG = -1e30

f32 = jnp.float32
bf16 = jnp.bfloat16
LAST = (((1,), (1,)), ((), ()))


def layer_norm(x):
    mean = jnp.mean(x, axis=-1, keepdims=True)
    centred = x - mean
    var = jnp.mean(centred * centred, axis=-1, keepdims=True)
    return centred * lax.rsqrt(var + 1e-06)


def matmul(a, b):
    return jnp.dot(a, b, preferred_element_type=f32)


def kernel(
    tokens, tissue, dw, w1, w2, scale, wq, wk, wv, wo, out,
    tok, tis, dwv, dwf, w1v, w2v, scv, wqv, wkv, wvv, wov,
    halo, thalo, ext, conv, sec, xbuf, k_all, v_all, qblk,
    s_ref, p_ref, m_ref, l_ref, a_ref, acc,
    load_sem, misc_s, misc_r, ring_s, ring_r, par_s, par_r,
):
    me = lax.axis_index("tile")
    core = lax.rem(me, 2)
    z = lax.rem(lax.div(me, 2), 8)
    y = lax.div(me, 16)
    partner = me + 1 - 2 * core
    zup = y * 16 + lax.rem(z + 1, 8) * 2 + core
    zdn = y * 16 + lax.rem(z + 7, 8) * 2 + core
    yoth = (1 - y) * 16 + z * 2 + core
    upper = lax.rem(me + 1, 32)
    lower = lax.rem(me + 31, 32)
    beyond = lower + core * (upper - lower)
    nxt = zup + core * (zdn - zup)
    half = pl.ds(pl.multiple_of(core * UNIT, UNIT), UNIT)

    pairs = [(tokens, tok), (tissue, tis), (dw, dwv), (w1, w1v), (w2, w2v), (scale, scv),
             (wq, wqv), (wk, wkv), (wv, wvv), (wo, wov)]
    loads = [pltpu.make_async_copy(a, b, load_sem.at[i]) for i, (a, b) in enumerate(pairs)]
    for load in loads:
        load.start()

    barrier = pltpu.get_barrier_semaphore()
    for other in (partner, zup, zdn, yoth, beyond):
        pl.semaphore_signal(barrier, inc=1, device_id={"tile": other},
                            device_id_type=pl.DeviceIdType.MESH)
    pl.semaphore_wait(barrier, 5)

    def remote(src, dst, send, recv, device):
        return pltpu.make_async_remote_copy(
            src_ref=src, dst_ref=dst, send_sem=send, recv_sem=recv,
            device_id={"tile": device}, device_id_type=pl.DeviceIdType.MESH)

    def misc(src, dst, i, device):
        return remote(src, dst, misc_s.at[i], misc_r.at[i], device)

    halos = [
        misc(tokens, halo.at[0], 0, upper), misc(tokens, halo.at[1], 1, lower),
        misc(tissue, thalo.at[0], 2, upper), misc(tissue, thalo.at[1], 3, lower),
    ]
    for copy in halos:
        copy.start()

    eye = lax.broadcasted_iota(jnp.int32, (GW, GW), 0) == lax.broadcasted_iota(jnp.int32, (GW, GW), 1)

    def column(row):
        return jnp.sum(jnp.where(eye, row.astype(f32), 0.0), axis=1, keepdims=True)

    col_ids = lax.broadcasted_iota(jnp.int32, (GW, 128), 0)

    def conv_pass(rows, first):
        @pl.loop(0, C // 128)
        def _(tile):
            lanes = pl.ds(pl.multiple_of(tile * 128, 128), 128)
            for r in range(ROWS):
                total = None
                for j in range(7):
                    part = None
                    for i in range(7):
                        if r + i in rows:
                            term = ext[r + i, :, lanes] * dwf[i, pl.ds(j, 1), lanes]
                            part = term if part is None else part + term
                    if part is None:
                        continue
                    s = j - 3
                    if s:
                        moved = pltpu.roll(part, (-s) % GW, 0)
                        inside = (col_ids + s >= 0) & (col_ids + s < GW)
                        part = jnp.where(inside, moved, 0.0)
                    total = part if total is None else total + part
                where = pl.ds(r * GW, GW)
                conv[where, lanes] = total if first else conv[where, lanes] + total

    for i in range(3):
        loads[i].wait()
    dwf[...] = dwv[...].astype(f32)
    for r in range(ROWS):
        ext[3 + r] = tok[r].astype(f32) * column(tis[r : r + 1, :])
    conv_pass((3, 4, 5), True)
    for copy in halos:
        copy.wait_recv()
    has_low = jnp.where(me > 0, 1.0, 0.0)
    has_high = jnp.where(me < 31, 1.0, 0.0)
    for r in range(ROWS):
        ext[r] = halo[0, r].astype(f32) * (column(thalo[0, r : r + 1, :]) * has_low)
        ext[6 + r] = halo[1, r].astype(f32) * (column(thalo[1, r : r + 1, :]) * has_high)
    conv_pass((0, 1, 2, 6, 7, 8), False)

    normed1 = layer_norm(conv[...]).astype(bf16)
    for i in range(3, 6):
        loads[i].wait()
    branch = None
    for n in range(3):
        cut = slice(n * 512, (n + 1) * 512)
        h = matmul(normed1, w1v[:, cut])
        h = (0.5 * h * (1.0 + lax.erf(h * 0.7071067811865476))).astype(bf16)
        part = matmul(h, w2v[cut, :])
        branch = part if branch is None else branch + part
    masked = ext[3:6].reshape(TOK, C)
    section = (masked + scv[...][None, :] * branch).astype(bf16)
    sec[...] = section
    normed2 = layer_norm(section.astype(f32)).astype(bf16)

    flags = tis[...].astype(f32)
    before = lax.broadcasted_iota(jnp.int32, (GW, GW), 0) < lax.broadcasted_iota(jnp.int32, (GW, GW), 1)
    rank = matmul(flags.astype(bf16), jnp.where(before, 1.0, 0.0).astype(bf16))
    counts = jnp.sum(flags, axis=1, keepdims=True)
    slot = lax.broadcasted_iota(jnp.int32, (CAP, GW), 0).astype(f32)
    x = jnp.zeros((CAP, C), f32)
    offset = jnp.zeros((1, 1), f32)
    for r in range(ROWS):
        pick = (slot == rank[r : r + 1, :] + offset) & (flags[r : r + 1, :] > 0)
        x = x + matmul(jnp.where(pick, 1.0, 0.0).astype(bf16), normed2[r * GW : (r + 1) * GW, :])
        offset = offset + counts[r : r + 1, :]
    empty = (lax.broadcasted_iota(jnp.int32, (CAP, C), 0).astype(f32) >= offset) & (
        lax.broadcasted_iota(jnp.int32, (CAP, C), 1) == 0)
    x = jnp.where(empty, MARK, x).astype(bf16)

    own = xbuf.at[0, pl.ds(pl.multiple_of(core * CAP, CAP), CAP)]
    far = xbuf.at[0, pl.ds(pl.multiple_of(UNIT + core * CAP, CAP), CAP)]
    xbuf[0, pl.ds(pl.multiple_of(core * CAP, CAP), CAP), :] = x
    own_copy = misc(own, own, 4, partner)
    far_copy = misc(own, far, 5, yoth)
    far_share = misc(far, far, 6, partner)
    own_copy.start()
    far_copy.start()

    def ring(src, dst):
        return remote(xbuf.at[src, half], xbuf.at[dst, half], ring_s.at[dst], ring_r.at[dst], nxt)

    def share(c):
        return remote(xbuf.at[c, half], xbuf.at[c, half], par_s.at[c], par_r.at[c], partner)

    def first_ring(unit, dst):
        return remote(xbuf.at[0, pl.ds(unit * UNIT, UNIT)], xbuf.at[dst, half],
                      ring_s.at[dst], ring_r.at[dst], nxt)

    own_copy.wait_recv()
    first_ring(0, 1).start()

    loads[6].wait()
    lane = lax.broadcasted_iota(jnp.int32, (TOK, QW), 1)
    for g in range(QUADS):
        query = matmul(normed2, wqv[:, g * QW : (g + 1) * QW]).astype(bf16).astype(f32) * 0.125
        for h in range(4):
            mine = (lane >= h * HD) & (lane < (h + 1) * HD)
            qblk[g, h * TOK : (h + 1) * TOK, :] = jnp.where(mine, query, 0.0).astype(bf16)
    m_ref[...] = jnp.full(m_ref.shape, NEG, f32)
    l_ref[...] = jnp.zeros(l_ref.shape, f32)
    acc[...] = jnp.zeros(acc.shape, f32)

    far_copy.wait_recv()
    far_share.start()
    far_share.wait_recv()
    first_ring(1, 2).start()
    loads[7].wait()
    loads[8].wait()

    first_lane = jnp.where(lax.broadcasted_iota(jnp.int32, (8, C), 1) == 0, 1.0, 0.0).astype(bf16)

    def project(p):
        rows = pl.ds(pl.multiple_of(p * KS, KS), KS)
        xc = xbuf[pl.ds(2 * p, 2)].reshape(KS, C)
        for n in range(4):
            cut = slice(n * 256, (n + 1) * 256)
            k_all[rows, cut] = matmul(xc, wkv[:, cut]).astype(bf16)
            v_all[rows, cut] = matmul(xc, wvv[:, cut]).astype(bf16)

    ring(0, 1).wait_recv()
    ring(1, 3).start()
    share(1).start()
    share(1).wait_recv()
    project(0)

    half_lane = lax.broadcasted_iota(jnp.int32, (TOK, 128), 1) < HD

    def scores(p, g):
        rows = pl.ds(pl.multiple_of(p * KS, KS), KS)
        s_ref[g % 2] = lax.dot_general(
            qblk[g], k_all[rows, g * QW : (g + 1) * QW], LAST, preferred_element_type=f32)

    def attend(p, g, shift):
        at = g % 2
        tiles = range(KS // 128)
        for r in range(0, 4 * TOK, 32):
            rs = slice(r, r + 32)
            st = [
                (s_ref[at, rs, t * 128 : (t + 1) * 128].reshape(4, 8, 128)
                 + shift[:, t * 128 : (t + 1) * 128][None]).reshape(32, 128)
                for t in tiles
            ]
            top = functools.reduce(jnp.maximum, st)
            old = m_ref[g, rs, :]
            new = jnp.maximum(old, jnp.max(top, axis=1, keepdims=True))
            factor = jnp.exp(old - new)
            m_ref[g, rs, :] = new
            a_ref[at, rs, :] = factor
            total = None
            for t in tiles:
                weight = jnp.exp(st[t] - new)
                p_ref[at, rs, t * 128 : (t + 1) * 128] = weight.astype(bf16)
                total = weight if total is None else total + weight
            l_ref[g, rs, :] = l_ref[g, rs, :] * factor + total
        rows = pl.ds(pl.multiple_of(p * KS, KS), KS)
        o = matmul(p_ref[at], v_all[rows, g * QW : (g + 1) * QW])
        for t in range(2):
            a, b = slice(2 * t * TOK, (2 * t + 1) * TOK), slice((2 * t + 1) * TOK, (2 * t + 2) * TOK)
            cut = slice(t * 128, (t + 1) * 128)
            o_t = jnp.where(half_lane, o[a, cut], o[b, cut])
            f_t = jnp.where(half_lane, a_ref[at, a, :], a_ref[at, b, :])
            dst = slice(g * QW + t * 128, g * QW + (t + 1) * 128)
            acc[:, dst] = acc[:, dst] * f_t + o_t

    def mask(p):
        marks = [
            lax.dot_general(first_lane, xbuf[2 * p + i], LAST, preferred_element_type=f32) for i in range(2)
        ]
        return jnp.where(jnp.concatenate(marks, axis=1) > 0.5 * MARK, NEG, 0.0)

    scores(0, 0)

    @pl.loop(0, 3)
    def _(p):
        even, odd = 2 * p + 2, 2 * p + 3
        last = lax.div(p, 2)
        shift = mask(p)
        scores(p, 1)
        attend(p, 0, shift)
        ring(even, even).wait_recv()
        share(even).start()
        ring(even + last * (core - 1), even + 2 - last).start()
        scores(p, 2)
        attend(p, 1, shift)
        ring(odd, odd).wait_recv()
        share(odd).start()

        @pl.when(p == 0)
        def _():
            ring(odd, odd + 2).start()

        scores(p, 3)
        attend(p, 2, shift)
        share(even).wait_recv()
        share(odd).wait_recv()
        project(p + 1)
        scores(p + 1, 0)
        attend(p, 3, shift)

    shift = mask(3)
    for g in range(QUADS):
        if g < 3:
            scores(3, g + 1)
        attend(3, g, shift)

    loads[9].wait()
    result = sec[...].astype(f32)
    for g in range(QUADS):
        parts = []
        for t in range(2):
            a, b = slice(2 * t * TOK, (2 * t + 1) * TOK), slice((2 * t + 1) * TOK, (2 * t + 2) * TOK)
            total_a = jnp.sum(l_ref[g, a, :], axis=1, keepdims=True)
            total_b = jnp.sum(l_ref[g, b, :], axis=1, keepdims=True)
            dst = slice(g * QW + t * 128, g * QW + (t + 1) * 128)
            parts.append((acc[:, dst] / jnp.where(half_lane, total_a, total_b)).astype(bf16))
        result = result + matmul(jnp.concatenate(parts, axis=1), wov[g * QW : (g + 1) * QW, :])
    out[...] = result.astype(bf16).reshape(ROWS, GW, C)

    for copy in halos + [own_copy, far_copy, far_share]:
        copy.wait_send()
    for c in range(1, NCHUNK):
        ring(c, c).wait_send()
        share(c).wait_send()


def local(tokens, tissue, dw_kernel, w_fc1, w_fc2, layer_scale, w_query, w_key, w_value, w_out):
    vmem, sem = pltpu.VMEM, pltpu.SemaphoreType.DMA
    return pl.pallas_call(
        kernel,
        out_shape=jax.ShapeDtypeStruct((ROWS, GW, C), bf16),
        in_specs=[pl.BlockSpec(memory_space=pl.ANY)] * 10,
        out_specs=pl.BlockSpec(memory_space=pltpu.VMEM),
        scratch_shapes=[
            vmem((ROWS, GW, C), bf16), vmem((ROWS, GW), jnp.int32),
            vmem((7, 7, C), bf16), vmem((7, 7, C), f32),
            vmem((C, HID), bf16), vmem((HID, C), bf16), vmem((C,), f32),
            vmem((C, 1024), bf16), vmem((C, 1024), bf16), vmem((C, 1024), bf16), vmem((1024, C), bf16),
            vmem((2, ROWS, GW, C), bf16), vmem((2, ROWS, GW), jnp.int32),
            vmem((9, GW, C), f32), vmem((TOK, C), f32), vmem((TOK, C), bf16),
            vmem((NCHUNK, CHUNK, C), bf16),
            vmem((NCHUNK * CHUNK, 1024), bf16), vmem((NCHUNK * CHUNK, 1024), bf16),
            vmem((QUADS, 4 * TOK, QW), bf16),
            vmem((2, 4 * TOK, KS), f32), vmem((2, 4 * TOK, KS), bf16),
            vmem((QUADS, 4 * TOK, 128), f32), vmem((QUADS, 4 * TOK, 128), f32),
            vmem((2, 4 * TOK, 128), f32), vmem((TOK, 1024), f32),
            sem((10,)), sem((7,)), sem((7,)), sem((NCHUNK,)), sem((NCHUNK,)), sem((NCHUNK,)), sem((NCHUNK,)),
        ],
        compiler_params=pltpu.CompilerParams(
            collective_id=0, has_side_effects=True, vmem_limit_bytes=60 << 20),
        name="block",
    )(tokens, tissue, dw_kernel, w_fc1, w_fc2, layer_scale, w_query, w_key, w_value, w_out)


def solution(mesh):
    spec = P(("slide", "tile"), None, None)
    in_specs = (spec, P(("slide", "tile"), None)) + (P(),) * 8
    return jax.shard_map(local, mesh=mesh, in_specs=in_specs, out_specs=spec, check_vma=False)
```

```python
import functools

import jax
import jax.numpy as jnp
from jax import lax
from jax.experimental import pallas as pl
from jax.experimental.pallas import tpu as pltpu
from jax.sharding import PartitionSpec as P

HEADS = 16
HD = 64
CAP = 96
ROWS = 3
GW = 64
C = 384
HID = 1536
TOK = ROWS * GW
UNIT = 2 * CAP
CHUNK = 4 * CAP
NCHUNK = 8
KS = 2 * CHUNK
GROUPS = 4
QW = 256
HALF = 512
MARK = 1024.0
NEG = -1e30

f32 = jnp.float32
bf16 = jnp.bfloat16
LAST = (((1,), (1,)), ((), ()))


def layer_norm(x):
    mean = jnp.mean(x, axis=-1, keepdims=True)
    centred = x - mean
    var = jnp.mean(centred * centred, axis=-1, keepdims=True)
    return centred * lax.rsqrt(var + 1e-06)


def matmul(a, b):
    return jnp.dot(a, b, preferred_element_type=f32)


def kernel(
    tokens, tissue, dw, w1, w2, scale, wq, wk, wv, wo, out,
    tok, tis, dwv, dwf, w1v, w2v, scv, wqv, wkv, wvv, wov,
    halo, thalo, ext, conv, sec, n2buf, xbuf, k_all, v_all, qblk,
    s_ref, p_ref, m_ref, l_ref, a_ref, acc, att_out, att_in,
    load_sem, misc_s, misc_r, ring_s, ring_r, par_s, par_r,
):
    me = lax.axis_index("tile")
    core = lax.rem(me, 2)
    z = lax.rem(lax.div(me, 2), 8)
    y = lax.div(me, 16)
    partner = me + 1 - 2 * core
    zup = y * 16 + lax.rem(z + 1, 8) * 2 + core
    zdn = y * 16 + lax.rem(z + 7, 8) * 2 + core
    yoth = (1 - y) * 16 + z * 2 + core
    upper = lax.rem(me + 1, 32)
    lower = lax.rem(me + 31, 32)
    beyond = lower + core * (upper - lower)
    nxt = zup + core * (zdn - zup)
    half = pl.ds(pl.multiple_of(core * UNIT, UNIT), UNIT)

    mine = pl.ds(pl.multiple_of(core * HALF, HALF), HALF)
    theirs = pl.ds(pl.multiple_of((1 - core) * HALF, HALF), HALF)
    pairs = [(tokens, tok), (tissue, tis), (dw, dwv), (w1, w1v), (w2, w2v), (scale, scv),
             (wq.at[:, mine], wqv), (wk.at[:, mine], wkv), (wv.at[:, mine], wvv),
             (wo.at[mine], wov.at[0]), (wo.at[theirs], wov.at[1])]
    loads = [pltpu.make_async_copy(a, b, load_sem.at[i]) for i, (a, b) in enumerate(pairs)]
    for load in loads:
        load.start()

    barrier = pltpu.get_barrier_semaphore()
    for other in (partner, zup, zdn, yoth, beyond):
        pl.semaphore_signal(barrier, inc=1, device_id={"tile": other},
                            device_id_type=pl.DeviceIdType.MESH)
    pl.semaphore_wait(barrier, 5)

    def remote(src, dst, send, recv, device):
        return pltpu.make_async_remote_copy(
            src_ref=src, dst_ref=dst, send_sem=send, recv_sem=recv,
            device_id={"tile": device}, device_id_type=pl.DeviceIdType.MESH)

    def misc(src, dst, i, device):
        return remote(src, dst, misc_s.at[i], misc_r.at[i], device)

    halos = [
        misc(tokens, halo.at[0], 0, upper), misc(tokens, halo.at[1], 1, lower),
        misc(tissue, thalo.at[0], 2, upper), misc(tissue, thalo.at[1], 3, lower),
    ]
    for copy in halos:
        copy.start()

    eye = lax.broadcasted_iota(jnp.int32, (GW, GW), 0) == lax.broadcasted_iota(jnp.int32, (GW, GW), 1)

    def column(row):
        return jnp.sum(jnp.where(eye, row.astype(f32), 0.0), axis=1, keepdims=True)

    col_ids = lax.broadcasted_iota(jnp.int32, (GW, 128), 0)

    def conv_pass(rows, first):
        @pl.loop(0, C // 128)
        def _(tile):
            lanes = pl.ds(pl.multiple_of(tile * 128, 128), 128)
            for r in range(ROWS):
                total = None
                for j in range(7):
                    part = None
                    for i in range(7):
                        if r + i in rows:
                            term = ext[r + i, :, lanes] * dwf[i, pl.ds(j, 1), lanes]
                            part = term if part is None else part + term
                    if part is None:
                        continue
                    s = j - 3
                    if s:
                        moved = pltpu.roll(part, (-s) % GW, 0)
                        inside = (col_ids + s >= 0) & (col_ids + s < GW)
                        part = jnp.where(inside, moved, 0.0)
                    total = part if total is None else total + part
                where = pl.ds(r * GW, GW)
                conv[where, lanes] = total if first else conv[where, lanes] + total

    for i in range(3):
        loads[i].wait()
    dwf[...] = dwv[...].astype(f32)
    for r in range(ROWS):
        ext[3 + r] = tok[r].astype(f32) * column(tis[r : r + 1, :])
    conv_pass((3, 4, 5), True)
    for copy in halos:
        copy.wait_recv()
    has_low = jnp.where(me > 0, 1.0, 0.0)
    has_high = jnp.where(me < 31, 1.0, 0.0)
    for r in range(ROWS):
        ext[r] = halo[0, r].astype(f32) * (column(thalo[0, r : r + 1, :]) * has_low)
        ext[6 + r] = halo[1, r].astype(f32) * (column(thalo[1, r : r + 1, :]) * has_high)
    conv_pass((0, 1, 2, 6, 7, 8), False)

    normed1 = layer_norm(conv[...]).astype(bf16)
    for i in range(3, 6):
        loads[i].wait()
    branch = None
    for n in range(3):
        cut = slice(n * 512, (n + 1) * 512)
        h = matmul(normed1, w1v[:, cut])
        h = (0.5 * h * (1.0 + lax.erf(h * 0.7071067811865476))).astype(bf16)
        part = matmul(h, w2v[cut, :])
        branch = part if branch is None else branch + part
    masked = ext[3:6].reshape(TOK, C)
    section = (masked + scv[...][None, :] * branch).astype(bf16)
    sec[...] = section
    normed2 = layer_norm(section.astype(f32)).astype(bf16)
    n2buf[1] = normed2

    flags = tis[...].astype(f32)
    before = lax.broadcasted_iota(jnp.int32, (GW, GW), 0) < lax.broadcasted_iota(jnp.int32, (GW, GW), 1)
    rank = matmul(flags.astype(bf16), jnp.where(before, 1.0, 0.0).astype(bf16))
    counts = jnp.sum(flags, axis=1, keepdims=True)
    slot = lax.broadcasted_iota(jnp.int32, (CAP, GW), 0).astype(f32)
    x = jnp.zeros((CAP, C), f32)
    offset = jnp.zeros((1, 1), f32)
    for r in range(ROWS):
        pick = (slot == rank[r : r + 1, :] + offset) & (flags[r : r + 1, :] > 0)
        x = x + matmul(jnp.where(pick, 1.0, 0.0).astype(bf16), normed2[r * GW : (r + 1) * GW, :])
        offset = offset + counts[r : r + 1, :]
    empty = (lax.broadcasted_iota(jnp.int32, (CAP, C), 0).astype(f32) >= offset) & (
        lax.broadcasted_iota(jnp.int32, (CAP, C), 1) == 0)
    x = jnp.where(empty, MARK, x).astype(bf16)

    own = xbuf.at[0, pl.ds(pl.multiple_of(core * CAP, CAP), CAP)]
    far = xbuf.at[0, pl.ds(pl.multiple_of(UNIT + core * CAP, CAP), CAP)]
    xbuf[0, pl.ds(pl.multiple_of(core * CAP, CAP), CAP), :] = x
    own_copy = misc(own, own, 4, partner)
    far_copy = misc(own, far, 5, yoth)
    far_share = misc(far, far, 6, partner)
    n2_copy = misc(n2buf.at[1], n2buf.at[0], 7, partner)
    att_copy = misc(att_out, att_in, 8, partner)
    own_copy.start()
    far_copy.start()
    n2_copy.start()

    def ring(src, dst):
        return remote(xbuf.at[src, half], xbuf.at[dst, half], ring_s.at[dst], ring_r.at[dst], nxt)

    def share(c):
        return remote(xbuf.at[c, half], xbuf.at[c, half], par_s.at[c], par_r.at[c], partner)

    def first_ring(unit, dst):
        return remote(xbuf.at[0, pl.ds(unit * UNIT, UNIT)], xbuf.at[dst, half],
                      ring_s.at[dst], ring_r.at[dst], nxt)

    own_copy.wait_recv()
    first_ring(0, 1).start()

    loads[6].wait()
    lane = lax.broadcasted_iota(jnp.int32, (TOK, QW), 1)

    def queries(group, normed):
        cut = slice((group % 2) * QW, (group % 2 + 1) * QW)
        query = matmul(normed, wqv[:, cut]).astype(bf16).astype(f32) * 0.125
        for h in range(4):
            inside = (lane >= h * HD) & (lane < (h + 1) * HD)
            qblk[group, h * TOK : (h + 1) * TOK, :] = jnp.where(inside, query, 0.0).astype(bf16)

    for group in (2, 3):
        queries(group, normed2)
    m_ref[...] = jnp.full(m_ref.shape, NEG, f32)
    l_ref[...] = jnp.zeros(l_ref.shape, f32)
    acc[...] = jnp.zeros(acc.shape, f32)

    far_copy.wait_recv()
    far_share.start()
    n2_copy.wait_recv()
    for group in (0, 1):
        queries(group, n2buf[0])
    far_share.wait_recv()
    first_ring(1, 2).start()
    loads[7].wait()
    loads[8].wait()

    first_lane = jnp.where(lax.broadcasted_iota(jnp.int32, (8, C), 1) == 0, 1.0, 0.0).astype(bf16)

    def project(p):
        rows = pl.ds(pl.multiple_of(p * KS, KS), KS)
        xc = xbuf[pl.ds(2 * p, 2)].reshape(KS, C)
        for n in range(2):
            cut = slice(n * 256, (n + 1) * 256)
            k_all[rows, cut] = matmul(xc, wkv[:, cut]).astype(bf16)
            v_all[rows, cut] = matmul(xc, wvv[:, cut]).astype(bf16)

    ring(0, 1).wait_recv()
    ring(1, 3).start()
    share(1).start()
    share(1).wait_recv()
    project(0)

    half_lane = lax.broadcasted_iota(jnp.int32, (TOK, 128), 1) < HD

    def scores(p, g):
        rows = pl.ds(pl.multiple_of(p * KS, KS), KS)
        s_ref[g % 2] = lax.dot_general(
            qblk[g], k_all[rows, (g % 2) * QW : (g % 2 + 1) * QW], LAST, preferred_element_type=f32)

    def attend(p, g, shift):
        at = g % 2
        tiles = range(KS // 128)
        for r in range(0, 4 * TOK, 32):
            rs = slice(r, r + 32)
            st = [
                (s_ref[at, rs, t * 128 : (t + 1) * 128].reshape(4, 8, 128)
                 + shift[:, t * 128 : (t + 1) * 128][None]).reshape(32, 128)
                for t in tiles
            ]
            top = functools.reduce(jnp.maximum, st)
            old = m_ref[g, rs, :]
            new = jnp.maximum(old, jnp.max(top, axis=1, keepdims=True))
            factor = jnp.exp(old - new)
            m_ref[g, rs, :] = new
            a_ref[at, rs, :] = factor
            total = None
            for t in tiles:
                weight = jnp.exp(st[t] - new)
                p_ref[at, rs, t * 128 : (t + 1) * 128] = weight.astype(bf16)
                total = weight if total is None else total + weight
            l_ref[g, rs, :] = l_ref[g, rs, :] * factor + total
        rows = pl.ds(pl.multiple_of(p * KS, KS), KS)
        o = matmul(p_ref[at], v_all[rows, (g % 2) * QW : (g % 2 + 1) * QW])
        for t in range(2):
            a, b = slice(2 * t * TOK, (2 * t + 1) * TOK), slice((2 * t + 1) * TOK, (2 * t + 2) * TOK)
            cut = slice(t * 128, (t + 1) * 128)
            o_t = jnp.where(half_lane, o[a, cut], o[b, cut])
            f_t = jnp.where(half_lane, a_ref[at, a, :], a_ref[at, b, :])
            dst = slice((g % 2) * QW + t * 128, (g % 2) * QW + (t + 1) * 128)
            acc[g // 2, :, dst] = acc[g // 2, :, dst] * f_t + o_t

    def mask(p):
        marks = [
            lax.dot_general(first_lane, xbuf[2 * p + i], LAST, preferred_element_type=f32) for i in range(2)
        ]
        return jnp.where(jnp.concatenate(marks, axis=1) > 0.5 * MARK, NEG, 0.0)

    scores(0, 0)

    @pl.loop(0, 3)
    def _(p):
        even, odd = 2 * p + 2, 2 * p + 3
        last = lax.div(p, 2)
        shift = mask(p)
        scores(p, 1)
        attend(p, 0, shift)
        ring(even, even).wait_recv()
        share(even).start()
        ring(even + last * (core - 1), even + 2 - last).start()
        scores(p, 2)
        attend(p, 1, shift)
        ring(odd, odd).wait_recv()
        share(odd).start()

        @pl.when(p == 0)
        def _():
            ring(odd, odd + 2).start()

        scores(p, 3)
        attend(p, 2, shift)
        share(even).wait_recv()
        share(odd).wait_recv()
        project(p + 1)
        scores(p + 1, 0)
        attend(p, 3, shift)

    def attended(who):
        parts = []
        for g in (2 * who, 2 * who + 1):
            for t in range(2):
                a, b = slice(2 * t * TOK, (2 * t + 1) * TOK), slice((2 * t + 1) * TOK, (2 * t + 2) * TOK)
                total_a = jnp.sum(l_ref[g, a, :], axis=1, keepdims=True)
                total_b = jnp.sum(l_ref[g, b, :], axis=1, keepdims=True)
                dst = slice((g % 2) * QW + t * 128, (g % 2) * QW + (t + 1) * 128)
                parts.append((acc[who, :, dst] / jnp.where(half_lane, total_a, total_b)).astype(bf16))
        return jnp.concatenate(parts, axis=1)

    shift = mask(3)
    scores(3, 1)
    attend(3, 0, shift)
    scores(3, 2)
    attend(3, 1, shift)
    att_out[...] = attended(0)
    att_copy.start()
    scores(3, 3)
    attend(3, 2, shift)
    attend(3, 3, shift)

    loads[9].wait()
    loads[10].wait()
    result = sec[...].astype(f32) + matmul(attended(1), wov[0])
    att_copy.wait_recv()
    result = result + matmul(att_in[...], wov[1])
    out[...] = result.astype(bf16).reshape(ROWS, GW, C)

    for copy in halos + [own_copy, far_copy, far_share, n2_copy, att_copy]:
        copy.wait_send()
    for c in range(1, NCHUNK):
        ring(c, c).wait_send()
        share(c).wait_send()


def local(tokens, tissue, dw_kernel, w_fc1, w_fc2, layer_scale, w_query, w_key, w_value, w_out):
    vmem, sem = pltpu.VMEM, pltpu.SemaphoreType.DMA
    return pl.pallas_call(
        kernel,
        out_shape=jax.ShapeDtypeStruct((ROWS, GW, C), bf16),
        in_specs=[pl.BlockSpec(memory_space=pl.ANY)] * 10,
        out_specs=pl.BlockSpec(memory_space=pltpu.VMEM),
        scratch_shapes=[
            vmem((ROWS, GW, C), bf16), vmem((ROWS, GW), jnp.int32),
            vmem((7, 7, C), bf16), vmem((7, 7, C), f32),
            vmem((C, HID), bf16), vmem((HID, C), bf16), vmem((C,), f32),
            vmem((C, HALF), bf16), vmem((C, HALF), bf16), vmem((C, HALF), bf16), vmem((2, HALF, C), bf16),
            vmem((2, ROWS, GW, C), bf16), vmem((2, ROWS, GW), jnp.int32),
            vmem((9, GW, C), f32), vmem((TOK, C), f32), vmem((TOK, C), bf16),
            vmem((2, TOK, C), bf16), vmem((NCHUNK, CHUNK, C), bf16),
            vmem((NCHUNK * CHUNK, HALF), bf16), vmem((NCHUNK * CHUNK, HALF), bf16),
            vmem((GROUPS, 4 * TOK, QW), bf16),
            vmem((2, 4 * TOK, KS), f32), vmem((2, 4 * TOK, KS), bf16),
            vmem((GROUPS, 4 * TOK, 128), f32), vmem((GROUPS, 4 * TOK, 128), f32),
            vmem((2, 4 * TOK, 128), f32), vmem((2, TOK, HALF), f32),
            vmem((TOK, HALF), bf16), vmem((TOK, HALF), bf16),
            sem((11,)), sem((9,)), sem((9,)), sem((NCHUNK,)), sem((NCHUNK,)), sem((NCHUNK,)), sem((NCHUNK,)),
        ],
        compiler_params=pltpu.CompilerParams(
            collective_id=0, has_side_effects=True, vmem_limit_bytes=60 << 20),
        name="block",
    )(tokens, tissue, dw_kernel, w_fc1, w_fc2, layer_scale, w_query, w_key, w_value, w_out)


def solution(mesh):
    spec = P(("slide", "tile"), None, None)
    in_specs = (spec, P(("slide", "tile"), None)) + (P(),) * 8
    return jax.shard_map(local, mesh=mesh, in_specs=in_specs, out_specs=spec, check_vma=False)
```

```python
import functools

import jax
import jax.numpy as jnp
from jax import lax
from jax.experimental import pallas as pl
from jax.experimental.pallas import tpu as pltpu
from jax.sharding import PartitionSpec as P

HEADS = 16
HD = 64
CAP = 96
ROWS = 3
GW = 64
C = 384
HID = 1536
TOK = ROWS * GW
UNIT = 2 * CAP
CHUNK = 4 * CAP
NCHUNK = 8
KS = 2 * CHUNK
GROUPS = 4
QW = 256
HALF = 512
MARK = 1024.0
NEG = -1e30

f32 = jnp.float32
bf16 = jnp.bfloat16
LAST = (((1,), (1,)), ((), ()))


def layer_norm(x):
    mean = jnp.mean(x, axis=-1, keepdims=True)
    centred = x - mean
    var = jnp.mean(centred * centred, axis=-1, keepdims=True)
    return centred * lax.rsqrt(var + 1e-06)


def matmul(a, b):
    return jnp.dot(a, b, preferred_element_type=f32)


def kernel(
    tokens, tissue, dw, w1, w2, scale, wq, wk, wv, wo, out,
    tok, tis, dwv, dwf, w1v, w2v, scv, wqv, wkv, wvv, wov,
    halo, thalo, ext, conv, sec, n2buf, xbuf, k_all, v_all, qblk,
    s_ref, p_ref, m_ref, l_ref, a_ref, acc, att_out, att_in,
    load_sem, misc_s, misc_r, ring_s, ring_r, par_s, par_r,
):
    me = lax.axis_index("tile")
    core = lax.rem(me, 2)
    z = lax.rem(lax.div(me, 2), 8)
    y = lax.div(me, 16)
    partner = me + 1 - 2 * core
    zup = y * 16 + lax.rem(z + 1, 8) * 2 + core
    zdn = y * 16 + lax.rem(z + 7, 8) * 2 + core
    yoth = (1 - y) * 16 + z * 2 + core
    upper = lax.rem(me + 1, 32)
    lower = lax.rem(me + 31, 32)
    beyond = lower + core * (upper - lower)
    along = (zup, zdn)

    mine = pl.ds(pl.multiple_of(core * HALF, HALF), HALF)
    theirs = pl.ds(pl.multiple_of((1 - core) * HALF, HALF), HALF)
    pairs = [(tokens, tok), (tissue, tis), (dw, dwv), (w1, w1v), (w2, w2v), (scale, scv),
             (wq.at[:, mine], wqv), (wk.at[:, mine], wkv), (wv.at[:, mine], wvv),
             (wo.at[mine], wov.at[0]), (wo.at[theirs], wov.at[1])]
    loads = [pltpu.make_async_copy(a, b, load_sem.at[i]) for i, (a, b) in enumerate(pairs)]
    for load in loads[:3]:
        load.start()

    barrier = pltpu.get_barrier_semaphore()
    for other in (partner, zup, zdn, yoth, beyond):
        pl.semaphore_signal(barrier, inc=1, device_id={"tile": other},
                            device_id_type=pl.DeviceIdType.MESH)
    pl.semaphore_wait(barrier, 5)

    def remote(src, dst, send, recv, device):
        return pltpu.make_async_remote_copy(
            src_ref=src, dst_ref=dst, send_sem=send, recv_sem=recv,
            device_id={"tile": device}, device_id_type=pl.DeviceIdType.MESH)

    def misc(src, dst, i, device):
        return remote(src, dst, misc_s.at[i], misc_r.at[i], device)

    halos = [
        misc(tokens, halo.at[0], 0, upper), misc(tokens, halo.at[1], 1, lower),
        misc(tissue, thalo.at[0], 2, upper), misc(tissue, thalo.at[1], 3, lower),
    ]
    for copy in halos:
        copy.start()
    for load in loads[3:]:
        load.start()

    eye = lax.broadcasted_iota(jnp.int32, (GW, GW), 0) == lax.broadcasted_iota(jnp.int32, (GW, GW), 1)

    def column(row):
        return jnp.sum(jnp.where(eye, row.astype(f32), 0.0), axis=1, keepdims=True)

    col_ids = lax.broadcasted_iota(jnp.int32, (GW, 128), 0)

    def conv_pass(rows, first):
        @pl.loop(0, C // 128)
        def _(tile):
            lanes = pl.ds(pl.multiple_of(tile * 128, 128), 128)
            for r in range(ROWS):
                total = None
                for j in range(7):
                    part = None
                    for i in range(7):
                        if r + i in rows:
                            term = ext[r + i, :, lanes] * dwf[i, pl.ds(j, 1), lanes]
                            part = term if part is None else part + term
                    if part is None:
                        continue
                    s = j - 3
                    if s:
                        moved = pltpu.roll(part, (-s) % GW, 0)
                        inside = (col_ids + s >= 0) & (col_ids + s < GW)
                        part = jnp.where(inside, moved, 0.0)
                    total = part if total is None else total + part
                where = pl.ds(r * GW, GW)
                conv[where, lanes] = total if first else conv[where, lanes] + total

    for i in range(3):
        loads[i].wait()
    dwf[...] = dwv[...].astype(f32)
    for r in range(ROWS):
        ext[3 + r] = tok[r].astype(f32) * column(tis[r : r + 1, :])
    conv_pass((3, 4, 5), True)
    for copy in halos:
        copy.wait_recv()
    has_low = jnp.where(me > 0, 1.0, 0.0)
    has_high = jnp.where(me < 31, 1.0, 0.0)
    for r in range(ROWS):
        ext[r] = halo[0, r].astype(f32) * (column(thalo[0, r : r + 1, :]) * has_low)
        ext[6 + r] = halo[1, r].astype(f32) * (column(thalo[1, r : r + 1, :]) * has_high)
    conv_pass((0, 1, 2, 6, 7, 8), False)

    normed1 = layer_norm(conv[...]).astype(bf16)
    for i in range(3, 6):
        loads[i].wait()
    branch = None
    for n in range(3):
        cut = slice(n * 512, (n + 1) * 512)
        h = matmul(normed1, w1v[:, cut])
        h = (0.5 * h * (1.0 + lax.erf(h * 0.7071067811865476))).astype(bf16)
        part = matmul(h, w2v[cut, :])
        branch = part if branch is None else branch + part
    masked = ext[3:6].reshape(TOK, C)
    section = (masked + scv[...][None, :] * branch).astype(bf16)
    sec[...] = section
    normed2 = layer_norm(section.astype(f32)).astype(bf16)
    n2buf[1] = normed2

    flags = tis[...].astype(f32)
    before = lax.broadcasted_iota(jnp.int32, (GW, GW), 0) < lax.broadcasted_iota(jnp.int32, (GW, GW), 1)
    rank = matmul(flags.astype(bf16), jnp.where(before, 1.0, 0.0).astype(bf16))
    counts = jnp.sum(flags, axis=1, keepdims=True)
    slot = lax.broadcasted_iota(jnp.int32, (CAP, GW), 0).astype(f32)
    x = jnp.zeros((CAP, C), f32)
    offset = jnp.zeros((1, 1), f32)
    for r in range(ROWS):
        pick = (slot == rank[r : r + 1, :] + offset) & (flags[r : r + 1, :] > 0)
        x = x + matmul(jnp.where(pick, 1.0, 0.0).astype(bf16), normed2[r * GW : (r + 1) * GW, :])
        offset = offset + counts[r : r + 1, :]
    empty = (lax.broadcasted_iota(jnp.int32, (CAP, C), 0).astype(f32) >= offset) & (
        lax.broadcasted_iota(jnp.int32, (CAP, C), 1) == 0)
    x = jnp.where(empty, MARK, x).astype(bf16)

    own = xbuf.at[0, pl.ds(pl.multiple_of(core * CAP, CAP), CAP)]
    far = xbuf.at[0, pl.ds(pl.multiple_of(UNIT + core * CAP, CAP), CAP)]
    xbuf[0, pl.ds(pl.multiple_of(core * CAP, CAP), CAP), :] = x
    own_copy = misc(own, own, 4, partner)
    far_copy = misc(own, far, 5, yoth)
    far_share = misc(far, far, 6, partner)
    n2_copy = misc(n2buf.at[1], n2buf.at[0], 7, partner)
    att_copy = misc(att_out, att_in, 8, partner)

    def block(c, way):
        return xbuf.at[c, pl.ds(pl.multiple_of(way * UNIT + core * CAP, CAP), CAP)]

    def hop(src, way, dst):
        at = way * NCHUNK + dst
        return remote(src, block(dst, way), ring_s.at[at], ring_r.at[at], along[way])

    def ring(way, src, dst):
        return hop(block(src, way), way, dst)

    def share(way, c):
        at = way * NCHUNK + c
        return remote(block(c, way), block(c, way), par_s.at[at], par_r.at[at], partner)

    for way in range(2):
        hop(own, way, 1).start()
    far_copy.start()
    own_copy.start()
    n2_copy.start()

    loads[6].wait()
    lane = lax.broadcasted_iota(jnp.int32, (TOK, QW), 1)

    def queries(group, normed):
        cut = slice((group % 2) * QW, (group % 2 + 1) * QW)
        query = matmul(normed, wqv[:, cut]).astype(bf16).astype(f32) * 0.125
        for h in range(4):
            inside = (lane >= h * HD) & (lane < (h + 1) * HD)
            qblk[group, h * TOK : (h + 1) * TOK, :] = jnp.where(inside, query, 0.0).astype(bf16)

    for group in (2, 3):
        queries(group, normed2)
    m_ref[...] = jnp.full(m_ref.shape, NEG, f32)
    l_ref[...] = jnp.zeros(l_ref.shape, f32)
    acc[...] = jnp.zeros(acc.shape, f32)

    n2_copy.wait_recv()
    for group in (0, 1):
        queries(group, n2buf[0])
    for way in range(2):
        ring(way, 1, 1).wait_recv()
        ring(way, 1, 3).start()
        share(way, 1).start()
    far_copy.wait_recv()
    far_share.start()
    for way in range(2):
        hop(far, way, 2).start()
    loads[7].wait()
    loads[8].wait()

    first_lane = jnp.where(lax.broadcasted_iota(jnp.int32, (8, C), 1) == 0, 1.0, 0.0).astype(bf16)

    def project(p):
        rows = pl.ds(pl.multiple_of(p * KS, KS), KS)
        xc = xbuf[pl.ds(2 * p, 2)].reshape(KS, C)
        for n in range(2):
            cut = slice(n * 256, (n + 1) * 256)
            k_all[rows, cut] = matmul(xc, wkv[:, cut]).astype(bf16)
            v_all[rows, cut] = matmul(xc, wvv[:, cut]).astype(bf16)

    own_copy.wait_recv()
    for way in range(2):
        share(way, 1).wait_recv()
    far_share.wait_recv()
    project(0)

    half_lane = lax.broadcasted_iota(jnp.int32, (TOK, 128), 1) < HD

    def scores(p, g):
        rows = pl.ds(pl.multiple_of(p * KS, KS), KS)
        s_ref[g % 2] = lax.dot_general(
            qblk[g], k_all[rows, (g % 2) * QW : (g % 2 + 1) * QW], LAST, preferred_element_type=f32)

    def attend(p, g, shift):
        at = g % 2
        tiles = range(KS // 128)
        for r in range(0, 4 * TOK, 32):
            rs = slice(r, r + 32)
            st = [
                (s_ref[at, rs, t * 128 : (t + 1) * 128].reshape(4, 8, 128)
                 + shift[:, t * 128 : (t + 1) * 128][None]).reshape(32, 128)
                for t in tiles
            ]
            top = functools.reduce(jnp.maximum, st)
            old = m_ref[g, rs, :]
            new = jnp.maximum(old, jnp.max(top, axis=1, keepdims=True))
            factor = jnp.exp(old - new)
            m_ref[g, rs, :] = new
            a_ref[at, rs, :] = factor
            total = None
            for t in tiles:
                weight = jnp.exp(st[t] - new)
                p_ref[at, rs, t * 128 : (t + 1) * 128] = weight.astype(bf16)
                total = weight if total is None else total + weight
            l_ref[g, rs, :] = l_ref[g, rs, :] * factor + total
        rows = pl.ds(pl.multiple_of(p * KS, KS), KS)
        o = matmul(p_ref[at], v_all[rows, (g % 2) * QW : (g % 2 + 1) * QW])
        for t in range(2):
            a, b = slice(2 * t * TOK, (2 * t + 1) * TOK), slice((2 * t + 1) * TOK, (2 * t + 2) * TOK)
            cut = slice(t * 128, (t + 1) * 128)
            o_t = jnp.where(half_lane, o[a, cut], o[b, cut])
            f_t = jnp.where(half_lane, a_ref[at, a, :], a_ref[at, b, :])
            dst = slice((g % 2) * QW + t * 128, (g % 2) * QW + (t + 1) * 128)
            acc[g // 2, :, dst] = acc[g // 2, :, dst] * f_t + o_t

    def mask(p):
        marks = [
            lax.dot_general(first_lane, xbuf[2 * p + i], LAST, preferred_element_type=f32) for i in range(2)
        ]
        return jnp.where(jnp.concatenate(marks, axis=1) > 0.5 * MARK, NEG, 0.0)

    scores(0, 0)

    @pl.loop(0, 3)
    def _(p):
        even, odd = 2 * p + 2, 2 * p + 3
        last = lax.div(p, 2)
        shift = mask(p)
        scores(p, 1)
        attend(p, 0, shift)
        for way in range(2):
            ring(way, even, even).wait_recv()
            ring(way, even - last * (1 - way), even + 2 - last).start()
            share(way, even).start()
        scores(p, 2)
        attend(p, 1, shift)
        for way in range(2):
            ring(way, odd, odd).wait_recv()
            share(way, odd).start()

        @pl.when(p == 0)
        def _():
            for way in range(2):
                ring(way, odd, odd + 2).start()

        scores(p, 3)
        attend(p, 2, shift)
        for way in range(2):
            share(way, even).wait_recv()
            share(way, odd).wait_recv()
        project(p + 1)
        scores(p + 1, 0)
        attend(p, 3, shift)

    def attended(who):
        parts = []
        for g in (2 * who, 2 * who + 1):
            for t in range(2):
                a, b = slice(2 * t * TOK, (2 * t + 1) * TOK), slice((2 * t + 1) * TOK, (2 * t + 2) * TOK)
                total_a = jnp.sum(l_ref[g, a, :], axis=1, keepdims=True)
                total_b = jnp.sum(l_ref[g, b, :], axis=1, keepdims=True)
                dst = slice((g % 2) * QW + t * 128, (g % 2) * QW + (t + 1) * 128)
                parts.append((acc[who, :, dst] / jnp.where(half_lane, total_a, total_b)).astype(bf16))
        return jnp.concatenate(parts, axis=1)

    shift = mask(3)
    scores(3, 1)
    attend(3, 0, shift)
    scores(3, 2)
    attend(3, 1, shift)
    att_out[...] = attended(0)
    att_copy.start()
    scores(3, 3)
    attend(3, 2, shift)
    attend(3, 3, shift)

    loads[9].wait()
    loads[10].wait()
    result = sec[...].astype(f32) + matmul(attended(1), wov[0])
    att_copy.wait_recv()
    result = result + matmul(att_in[...], wov[1])
    out[...] = result.astype(bf16).reshape(ROWS, GW, C)

    for copy in halos + [own_copy, far_copy, far_share, n2_copy, att_copy]:
        copy.wait_send()
    for c in range(1, NCHUNK):
        for way in range(2):
            ring(way, c, c).wait_send()
            share(way, c).wait_send()


def local(tokens, tissue, dw_kernel, w_fc1, w_fc2, layer_scale, w_query, w_key, w_value, w_out):
    vmem, sem = pltpu.VMEM, pltpu.SemaphoreType.DMA
    return pl.pallas_call(
        kernel,
        out_shape=jax.ShapeDtypeStruct((ROWS, GW, C), bf16),
        in_specs=[pl.BlockSpec(memory_space=pl.ANY)] * 10,
        out_specs=pl.BlockSpec(memory_space=pltpu.VMEM),
        scratch_shapes=[
            vmem((ROWS, GW, C), bf16), vmem((ROWS, GW), jnp.int32),
            vmem((7, 7, C), bf16), vmem((7, 7, C), f32),
            vmem((C, HID), bf16), vmem((HID, C), bf16), vmem((C,), f32),
            vmem((C, HALF), bf16), vmem((C, HALF), bf16), vmem((C, HALF), bf16), vmem((2, HALF, C), bf16),
            vmem((2, ROWS, GW, C), bf16), vmem((2, ROWS, GW), jnp.int32),
            vmem((9, GW, C), f32), vmem((TOK, C), f32), vmem((TOK, C), bf16),
            vmem((2, TOK, C), bf16), vmem((NCHUNK, CHUNK, C), bf16),
            vmem((NCHUNK * CHUNK, HALF), bf16), vmem((NCHUNK * CHUNK, HALF), bf16),
            vmem((GROUPS, 4 * TOK, QW), bf16),
            vmem((2, 4 * TOK, KS), f32), vmem((2, 4 * TOK, KS), bf16),
            vmem((GROUPS, 4 * TOK, 128), f32), vmem((GROUPS, 4 * TOK, 128), f32),
            vmem((2, 4 * TOK, 128), f32), vmem((2, TOK, HALF), f32),
            vmem((TOK, HALF), bf16), vmem((TOK, HALF), bf16),
            sem((11,)), sem((9,)), sem((9,)), sem((2 * NCHUNK,)), sem((2 * NCHUNK,)), sem((2 * NCHUNK,)), sem((2 * NCHUNK,)),
        ],
        compiler_params=pltpu.CompilerParams(
            collective_id=0, has_side_effects=True, vmem_limit_bytes=60 << 20),
        name="block",
    )(tokens, tissue, dw_kernel, w_fc1, w_fc2, layer_scale, w_query, w_key, w_value, w_out)


def solution(mesh):
    spec = P(("slide", "tile"), None, None)
    in_specs = (spec, P(("slide", "tile"), None)) + (P(),) * 8
    return jax.shard_map(local, mesh=mesh, in_specs=in_specs, out_specs=spec, check_vma=False)
```

```python
import functools

import jax
import jax.numpy as jnp
from jax import lax
from jax.experimental import pallas as pl
from jax.experimental.pallas import tpu as pltpu
from jax.sharding import PartitionSpec as P

HEADS = 16
HD = 64
CAP = 96
ROWS = 3
GW = 64
C = 384
HID = 1536
TOK = ROWS * GW
UNIT = 2 * CAP
CHUNK = 4 * CAP
NCHUNK = 8
KS = 2 * CHUNK
GROUPS = 4
QW = 256
HALF = 512
MARK = 1024.0
NEG = -1e30

f32 = jnp.float32
bf16 = jnp.bfloat16
LAST = (((1,), (1,)), ((), ()))


def layer_norm(x):
    mean = jnp.mean(x, axis=-1, keepdims=True)
    centred = x - mean
    var = jnp.mean(centred * centred, axis=-1, keepdims=True)
    return centred * lax.rsqrt(var + 1e-06)


def matmul(a, b):
    return jnp.dot(a, b, preferred_element_type=f32)


def kernel(
    tokens, tissue, dw, w1, w2, scale, wq, wk, wv, wo, out,
    tok, tis, dwv, dwf, w1v, w2v, scv, wqv, wkv, wvv, wov,
    halo, thalo, ext, conv, sec, n2buf, xbuf, k_all, v_all, qblk,
    s_ref, p_ref, m_ref, l_ref, a_ref, acc, att_out, att_in,
    load_sem, misc_s, misc_r, ring_s, ring_r, par_s, par_r,
):
    me = lax.axis_index("tile")
    core = lax.rem(me, 2)
    z = lax.rem(lax.div(me, 2), 8)
    y = lax.div(me, 16)
    partner = me + 1 - 2 * core
    zup = y * 16 + lax.rem(z + 1, 8) * 2 + core
    zdn = y * 16 + lax.rem(z + 7, 8) * 2 + core
    yoth = (1 - y) * 16 + z * 2 + core
    upper = lax.rem(me + 1, 32)
    lower = lax.rem(me + 31, 32)
    beyond = lower + core * (upper - lower)
    along = (zup, zdn)

    mine = pl.ds(pl.multiple_of(core * HALF, HALF), HALF)
    theirs = pl.ds(pl.multiple_of((1 - core) * HALF, HALF), HALF)
    pairs = [(tokens, tok), (tissue, tis), (dw, dwv), (w1, w1v), (w2, w2v), (scale, scv),
             (wq.at[:, mine], wqv), (wk.at[:, mine], wkv), (wv.at[:, mine], wvv),
             (wo.at[mine], wov.at[0]), (wo.at[theirs], wov.at[1])]
    loads = [pltpu.make_async_copy(a, b, load_sem.at[i]) for i, (a, b) in enumerate(pairs)]
    for load in loads[:3]:
        load.start()

    barrier = pltpu.get_barrier_semaphore()
    for other in (partner, zup, zdn, yoth, beyond):
        pl.semaphore_signal(barrier, inc=1, device_id={"tile": other},
                            device_id_type=pl.DeviceIdType.MESH)
    pl.semaphore_wait(barrier, 5)

    def remote(src, dst, send, recv, device):
        return pltpu.make_async_remote_copy(
            src_ref=src, dst_ref=dst, send_sem=send, recv_sem=recv,
            device_id={"tile": device}, device_id_type=pl.DeviceIdType.MESH)

    def misc(src, dst, i, device):
        return remote(src, dst, misc_s.at[i], misc_r.at[i], device)

    halos = [
        misc(tokens, halo.at[0], 0, upper), misc(tokens, halo.at[1], 1, lower),
        misc(tissue, thalo.at[0], 2, upper), misc(tissue, thalo.at[1], 3, lower),
    ]
    for copy in halos:
        copy.start()
    for load in loads[3:]:
        load.start()

    eye = lax.broadcasted_iota(jnp.int32, (GW, GW), 0) == lax.broadcasted_iota(jnp.int32, (GW, GW), 1)

    def column(row):
        return jnp.sum(jnp.where(eye, row.astype(f32), 0.0), axis=1, keepdims=True)

    col_ids = lax.broadcasted_iota(jnp.int32, (GW, 128), 0)

    def conv_pass(rows, first):
        @pl.loop(0, C // 128)
        def _(tile):
            lanes = pl.ds(pl.multiple_of(tile * 128, 128), 128)
            for r in range(ROWS):
                total = None
                for j in range(7):
                    part = None
                    for i in range(7):
                        if r + i in rows:
                            term = ext[r + i, :, lanes] * dwf[i, pl.ds(j, 1), lanes]
                            part = term if part is None else part + term
                    if part is None:
                        continue
                    s = j - 3
                    if s:
                        moved = pltpu.roll(part, (-s) % GW, 0)
                        inside = (col_ids + s >= 0) & (col_ids + s < GW)
                        part = jnp.where(inside, moved, 0.0)
                    total = part if total is None else total + part
                where = pl.ds(r * GW, GW)
                conv[where, lanes] = total if first else conv[where, lanes] + total

    for i in range(3):
        loads[i].wait()
    dwf[...] = dwv[...].astype(f32)
    for r in range(ROWS):
        ext[3 + r] = tok[r].astype(f32) * column(tis[r : r + 1, :])
    conv_pass((3, 4, 5), True)
    for copy in halos:
        copy.wait_recv()
    has_low = jnp.where(me > 0, 1.0, 0.0)
    has_high = jnp.where(me < 31, 1.0, 0.0)
    for r in range(ROWS):
        ext[r] = halo[0, r].astype(f32) * (column(thalo[0, r : r + 1, :]) * has_low)
        ext[6 + r] = halo[1, r].astype(f32) * (column(thalo[1, r : r + 1, :]) * has_high)
    conv_pass((0, 1, 2, 6, 7, 8), False)

    normed1 = layer_norm(conv[...]).astype(bf16)
    for i in range(3, 6):
        loads[i].wait()
    branch = None
    for n in range(3):
        cut = slice(n * 512, (n + 1) * 512)
        h = matmul(normed1, w1v[:, cut])
        h = (0.5 * h * (1.0 + lax.erf(h * 0.7071067811865476))).astype(bf16)
        part = matmul(h, w2v[cut, :])
        branch = part if branch is None else branch + part
    masked = ext[3:6].reshape(TOK, C)
    section = (masked + scv[...][None, :] * branch).astype(bf16)
    sec[...] = section
    normed2 = layer_norm(section.astype(f32)).astype(bf16)
    n2buf[1] = normed2

    flags = tis[...].astype(f32)
    before = lax.broadcasted_iota(jnp.int32, (GW, GW), 0) < lax.broadcasted_iota(jnp.int32, (GW, GW), 1)
    rank = matmul(flags.astype(bf16), jnp.where(before, 1.0, 0.0).astype(bf16))
    counts = jnp.sum(flags, axis=1, keepdims=True)
    slot = lax.broadcasted_iota(jnp.int32, (CAP, GW), 0).astype(f32)
    x = jnp.zeros((CAP, C), f32)
    offset = jnp.zeros((1, 1), f32)
    for r in range(ROWS):
        pick = (slot == rank[r : r + 1, :] + offset) & (flags[r : r + 1, :] > 0)
        x = x + matmul(jnp.where(pick, 1.0, 0.0).astype(bf16), normed2[r * GW : (r + 1) * GW, :])
        offset = offset + counts[r : r + 1, :]
    empty = (lax.broadcasted_iota(jnp.int32, (CAP, C), 0).astype(f32) >= offset) & (
        lax.broadcasted_iota(jnp.int32, (CAP, C), 1) == 0)
    x = jnp.where(empty, MARK, x).astype(bf16)

    own = xbuf.at[0, pl.ds(pl.multiple_of(core * CAP, CAP), CAP)]
    far = xbuf.at[0, pl.ds(pl.multiple_of(UNIT + core * CAP, CAP), CAP)]
    xbuf[0, pl.ds(pl.multiple_of(core * CAP, CAP), CAP), :] = x
    own_copy = misc(own, own, 4, partner)
    far_copy = misc(own, far, 5, yoth)
    far_share = misc(far, far, 6, partner)
    n2_copy = misc(n2buf.at[1], n2buf.at[0], 7, partner)
    att_copy = misc(att_out, att_in, 8, partner)

    def block(c, way):
        return xbuf.at[c, pl.ds(pl.multiple_of(way * UNIT + core * CAP, CAP), CAP)]

    def hop(src, way, dst):
        at = way * NCHUNK + dst
        return remote(src, block(dst, way), ring_s.at[at], ring_r.at[at], along[way])

    def ring(way, src, dst):
        return hop(block(src, way), way, dst)

    def share(way, c):
        at = way * NCHUNK + c
        return remote(block(c, way), block(c, way), par_s.at[at], par_r.at[at], partner)

    for way in range(2):
        hop(own, way, 1).start()
    far_copy.start()
    own_copy.start()
    n2_copy.start()

    loads[6].wait()
    lane = lax.broadcasted_iota(jnp.int32, (TOK, QW), 1)

    def queries(group, normed):
        cut = slice((group % 2) * QW, (group % 2 + 1) * QW)
        query = matmul(normed, wqv[:, cut]).astype(bf16).astype(f32) * 0.125
        for h in range(4):
            inside = (lane >= h * HD) & (lane < (h + 1) * HD)
            qblk[group, h * TOK : (h + 1) * TOK, :] = jnp.where(inside, query, 0.0).astype(bf16)

    for group in (2, 3):
        queries(group, normed2)
    m_ref[...] = jnp.full(m_ref.shape, NEG, f32)
    l_ref[...] = jnp.zeros(l_ref.shape, f32)
    acc[...] = jnp.zeros(acc.shape, f32)

    n2_copy.wait_recv()
    for group in (0, 1):
        queries(group, n2buf[0])
    for way in range(2):
        ring(way, 1, 1).wait_recv()
        ring(way, 1, 3).start()
        share(way, 1).start()
    far_copy.wait_recv()
    far_share.start()
    for way in range(2):
        hop(far, way, 2).start()
    loads[7].wait()
    loads[8].wait()

    first_lane = jnp.where(lax.broadcasted_iota(jnp.int32, (8, C), 1) == 0, 1.0, 0.0).astype(bf16)

    def project(p):
        rows = pl.ds(pl.multiple_of(p * KS, KS), KS)
        xc = xbuf[pl.ds(2 * p, 2)].reshape(KS, C)
        for n in range(2):
            cut = slice(n * 256, (n + 1) * 256)
            k_all[rows, cut] = matmul(xc, wkv[:, cut]).astype(bf16)
            v_all[rows, cut] = matmul(xc, wvv[:, cut]).astype(bf16)

    own_copy.wait_recv()
    for way in range(2):
        share(way, 1).wait_recv()
    far_share.wait_recv()
    project(0)

    half_lane = lax.broadcasted_iota(jnp.int32, (TOK, 128), 1) < HD

    def score_part(p, g, n):
        rows = pl.ds(pl.multiple_of(p * KS + n * 256, 256), 256)
        s_ref[g % 2, :, n * 256 : (n + 1) * 256] = lax.dot_general(
            qblk[g], k_all[rows, (g % 2) * QW : (g % 2 + 1) * QW], LAST, preferred_element_type=f32)

    def scores(p, g):
        for n in range(3):
            score_part(p, g, n)

    def weigh(p, g):
        at = g % 2
        rows = pl.ds(pl.multiple_of(p * KS, KS), KS)
        o = matmul(p_ref[at], v_all[rows, (g % 2) * QW : (g % 2 + 1) * QW])
        for t in range(2):
            a, b = slice(2 * t * TOK, (2 * t + 1) * TOK), slice((2 * t + 1) * TOK, (2 * t + 2) * TOK)
            cut = slice(t * 128, (t + 1) * 128)
            o_t = jnp.where(half_lane, o[a, cut], o[b, cut])
            f_t = jnp.where(half_lane, a_ref[at, a, :], a_ref[at, b, :])
            dst = slice((g % 2) * QW + t * 128, (g % 2) * QW + (t + 1) * 128)
            acc[g // 2, :, dst] = acc[g // 2, :, dst] * f_t + o_t

    def attend(p, g, shift, ahead=None, behind=None):
        at = g % 2
        tiles = range(KS // 128)
        for r in range(0, 4 * TOK, 32):
            rs = slice(r, r + 32)
            if ahead is not None and r % 256 == 0:
                score_part(*ahead, r // 256)
            if behind is not None and r == 128:
                weigh(*behind)
            st = [
                (s_ref[at, rs, t * 128 : (t + 1) * 128].reshape(4, 8, 128)
                 + shift[:, t * 128 : (t + 1) * 128][None]).reshape(32, 128)
                for t in tiles
            ]
            top = functools.reduce(jnp.maximum, st)
            old = m_ref[g, rs, :]
            new = jnp.maximum(old, jnp.max(top, axis=1, keepdims=True))
            factor = jnp.exp(old - new)
            m_ref[g, rs, :] = new
            a_ref[at, rs, :] = factor
            total = None
            for t in tiles:
                weight = jnp.exp(st[t] - new)
                p_ref[at, rs, t * 128 : (t + 1) * 128] = weight.astype(bf16)
                total = weight if total is None else total + weight
            l_ref[g, rs, :] = l_ref[g, rs, :] * factor + total
    def mask(p):
        marks = [
            lax.dot_general(first_lane, xbuf[2 * p + i], LAST, preferred_element_type=f32) for i in range(2)
        ]
        return jnp.where(jnp.concatenate(marks, axis=1) > 0.5 * MARK, NEG, 0.0)

    scores(0, 0)

    @pl.loop(0, 3)
    def _(p):
        even, odd = 2 * p + 2, 2 * p + 3
        shift = mask(p)

        def take_even():
            for way in range(2):
                ring(way, even, even).wait_recv()

            @pl.when(p < 2)
            def _():
                for way in range(2):
                    ring(way, even, even + 2).start()

            @pl.when(p == 2)
            def _():
                ring(1, even, 7).start()

            for way in range(2):
                share(way, even).start()

        pl.when(p > 0)(take_even)
        attend(p, 0, shift, (p, 1))
        pl.when(p == 0)(take_even)
        attend(p, 1, shift, (p, 2), (p, 0))
        for way in range(2):
            ring(way, odd, odd).wait_recv()

        @pl.when(p < 2)
        def _():
            ring(0, odd, odd + 2).start()

        @pl.when(p == 0)
        def _():
            ring(1, odd, odd + 2).start()

        for way in range(2):
            share(way, odd).start()

        attend(p, 2, shift, (p, 3), (p, 1))
        for way in range(2):
            share(way, even).wait_recv()
            share(way, odd).wait_recv()
        project(p + 1)
        attend(p, 3, shift, (p + 1, 0), (p, 2))
        weigh(p, 3)

    def attended(who):
        parts = []
        for g in (2 * who, 2 * who + 1):
            for t in range(2):
                a, b = slice(2 * t * TOK, (2 * t + 1) * TOK), slice((2 * t + 1) * TOK, (2 * t + 2) * TOK)
                total_a = jnp.sum(l_ref[g, a, :], axis=1, keepdims=True)
                total_b = jnp.sum(l_ref[g, b, :], axis=1, keepdims=True)
                dst = slice((g % 2) * QW + t * 128, (g % 2) * QW + (t + 1) * 128)
                parts.append((acc[who, :, dst] / jnp.where(half_lane, total_a, total_b)).astype(bf16))
        return jnp.concatenate(parts, axis=1)

    shift = mask(3)
    attend(3, 0, shift, (3, 1))
    attend(3, 1, shift, (3, 2), (3, 0))
    weigh(3, 1)
    att_out[...] = attended(0)
    att_copy.start()
    attend(3, 2, shift, (3, 3))
    attend(3, 3, shift, None, (3, 2))
    weigh(3, 3)

    loads[9].wait()
    loads[10].wait()
    result = sec[...].astype(f32) + matmul(attended(1), wov[0])
    att_copy.wait_recv()
    result = result + matmul(att_in[...], wov[1])
    out[...] = result.astype(bf16).reshape(ROWS, GW, C)

    for copy in halos + [own_copy, far_copy, far_share, n2_copy, att_copy]:
        copy.wait_send()
    for c in range(1, NCHUNK):
        for way in range(2):
            ring(way, c, c).wait_send()
            share(way, c).wait_send()


def local(tokens, tissue, dw_kernel, w_fc1, w_fc2, layer_scale, w_query, w_key, w_value, w_out):
    vmem, sem = pltpu.VMEM, pltpu.SemaphoreType.DMA
    return pl.pallas_call(
        kernel,
        out_shape=jax.ShapeDtypeStruct((ROWS, GW, C), bf16),
        in_specs=[pl.BlockSpec(memory_space=pl.ANY)] * 10,
        out_specs=pl.BlockSpec(memory_space=pltpu.VMEM),
        scratch_shapes=[
            vmem((ROWS, GW, C), bf16), vmem((ROWS, GW), jnp.int32),
            vmem((7, 7, C), bf16), vmem((7, 7, C), f32),
            vmem((C, HID), bf16), vmem((HID, C), bf16), vmem((C,), f32),
            vmem((C, HALF), bf16), vmem((C, HALF), bf16), vmem((C, HALF), bf16), vmem((2, HALF, C), bf16),
            vmem((2, ROWS, GW, C), bf16), vmem((2, ROWS, GW), jnp.int32),
            vmem((9, GW, C), f32), vmem((TOK, C), f32), vmem((TOK, C), bf16),
            vmem((2, TOK, C), bf16), vmem((NCHUNK, CHUNK, C), bf16),
            vmem((NCHUNK * CHUNK, HALF), bf16), vmem((NCHUNK * CHUNK, HALF), bf16),
            vmem((GROUPS, 4 * TOK, QW), bf16),
            vmem((2, 4 * TOK, KS), f32), vmem((2, 4 * TOK, KS), bf16),
            vmem((GROUPS, 4 * TOK, 128), f32), vmem((GROUPS, 4 * TOK, 128), f32),
            vmem((2, 4 * TOK, 128), f32), vmem((2, TOK, HALF), f32),
            vmem((TOK, HALF), bf16), vmem((TOK, HALF), bf16),
            sem((11,)), sem((9,)), sem((9,)), sem((2 * NCHUNK,)), sem((2 * NCHUNK,)), sem((2 * NCHUNK,)), sem((2 * NCHUNK,)),
        ],
        compiler_params=pltpu.CompilerParams(
            collective_id=0, has_side_effects=True, vmem_limit_bytes=60 << 20),
        name="block",
    )(tokens, tissue, dw_kernel, w_fc1, w_fc2, layer_scale, w_query, w_key, w_value, w_out)


def solution(mesh):
    spec = P(("slide", "tile"), None, None)
    in_specs = (spec, P(("slide", "tile"), None)) + (P(),) * 8
    return jax.shard_map(local, mesh=mesh, in_specs=in_specs, out_specs=spec, check_vma=False)
```

```python
import functools

import jax
import jax.numpy as jnp
from jax import lax
from jax.experimental import pallas as pl
from jax.experimental.pallas import tpu as pltpu
from jax.sharding import PartitionSpec as P

HEADS = 16
HD = 64
CAP = 96
ROWS = 3
GW = 64
C = 384
HID = 1536
TOK = ROWS * GW
UNIT = 2 * CAP
CHUNK = 4 * CAP
NCHUNK = 8
KS = 2 * CHUNK
GROUPS = 4
QW = 256
HALF = 512
MARK = 1024.0
NEG = -1e30

f32 = jnp.float32
bf16 = jnp.bfloat16
LAST = (((1,), (1,)), ((), ()))


def layer_norm(x):
    mean = jnp.mean(x, axis=-1, keepdims=True)
    centred = x - mean
    var = jnp.mean(centred * centred, axis=-1, keepdims=True)
    return centred * lax.rsqrt(var + 1e-06)


def matmul(a, b):
    return jnp.dot(a, b, preferred_element_type=f32)


def kernel(
    tokens, tissue, dw, w1, w2, scale, wq, wk, wv, wo, out,
    tok, tis, dwv, dwf, w1v, w2v, scv, wqv, wkv, wvv, wov,
    halo, thalo, ext, conv, sec, n2buf, xbuf, k_all, v_all, qblk,
    s_ref, p_ref, m_ref, l_ref, a_ref, acc, att_out, att_in,
    load_sem, misc_s, misc_r, ring_s, ring_r, par_s, par_r,
):
    me = lax.axis_index("tile")
    core = lax.rem(me, 2)
    z = lax.rem(lax.div(me, 2), 8)
    y = lax.div(me, 16)
    partner = me + 1 - 2 * core
    zup = y * 16 + lax.rem(z + 1, 8) * 2 + core
    zdn = y * 16 + lax.rem(z + 7, 8) * 2 + core
    yoth = (1 - y) * 16 + z * 2 + core
    upper = lax.rem(me + 1, 32)
    lower = lax.rem(me + 31, 32)
    beyond = lower + core * (upper - lower)
    along = (zup, zdn)

    mine = pl.ds(pl.multiple_of(core * HALF, HALF), HALF)
    theirs = pl.ds(pl.multiple_of((1 - core) * HALF, HALF), HALF)
    pairs = [(tokens, tok), (tissue, tis), (dw, dwv), (w1, w1v), (w2, w2v), (scale, scv),
             (wq.at[:, mine], wqv), (wk.at[:, mine], wkv), (wv.at[:, mine], wvv),
             (wo.at[mine], wov.at[0]), (wo.at[theirs], wov.at[1])]
    loads = [pltpu.make_async_copy(a, b, load_sem.at[i]) for i, (a, b) in enumerate(pairs)]
    for load in loads[:3]:
        load.start()

    barrier = pltpu.get_barrier_semaphore()
    for other in (partner, zup, zdn, yoth, beyond):
        pl.semaphore_signal(barrier, inc=1, device_id={"tile": other},
                            device_id_type=pl.DeviceIdType.MESH)
    pl.semaphore_wait(barrier, 5)

    def remote(src, dst, send, recv, device):
        return pltpu.make_async_remote_copy(
            src_ref=src, dst_ref=dst, send_sem=send, recv_sem=recv,
            device_id={"tile": device}, device_id_type=pl.DeviceIdType.MESH)

    def misc(src, dst, i, device):
        return remote(src, dst, misc_s.at[i], misc_r.at[i], device)

    halos = [
        misc(tokens, halo.at[0], 0, upper), misc(tokens, halo.at[1], 1, lower),
        misc(tissue, thalo.at[0], 2, upper), misc(tissue, thalo.at[1], 3, lower),
    ]
    for copy in halos:
        copy.start()
    for load in loads[3:]:
        load.start()

    eye = lax.broadcasted_iota(jnp.int32, (GW, GW), 0) == lax.broadcasted_iota(jnp.int32, (GW, GW), 1)

    def column(row):
        return jnp.sum(jnp.where(eye, row.astype(f32), 0.0), axis=1, keepdims=True)

    col_ids = lax.broadcasted_iota(jnp.int32, (GW, 128), 0)

    def conv_pass(rows, first):
        @pl.loop(0, C // 128)
        def _(tile):
            lanes = pl.ds(pl.multiple_of(tile * 128, 128), 128)
            for r in range(ROWS):
                total = None
                for j in range(7):
                    part = None
                    for i in range(7):
                        if r + i in rows:
                            term = ext[r + i, :, lanes] * dwf[i, pl.ds(j, 1), lanes]
                            part = term if part is None else part + term
                    if part is None:
                        continue
                    s = j - 3
                    if s:
                        moved = pltpu.roll(part, (-s) % GW, 0)
                        inside = (col_ids + s >= 0) & (col_ids + s < GW)
                        part = jnp.where(inside, moved, 0.0)
                    total = part if total is None else total + part
                where = pl.ds(r * GW, GW)
                conv[where, lanes] = total if first else conv[where, lanes] + total

    for i in range(3):
        loads[i].wait()
    dwf[...] = dwv[...].astype(f32)
    for r in range(ROWS):
        ext[3 + r] = tok[r].astype(f32) * column(tis[r : r + 1, :])
    conv_pass((3, 4, 5), True)
    for copy in halos:
        copy.wait_recv()
    has_low = jnp.where(me > 0, 1.0, 0.0)
    has_high = jnp.where(me < 31, 1.0, 0.0)
    for r in range(ROWS):
        ext[r] = halo[0, r].astype(f32) * (column(thalo[0, r : r + 1, :]) * has_low)
        ext[6 + r] = halo[1, r].astype(f32) * (column(thalo[1, r : r + 1, :]) * has_high)
    conv_pass((0, 1, 2, 6, 7, 8), False)

    normed1 = layer_norm(conv[...]).astype(bf16)
    for i in range(3, 6):
        loads[i].wait()
    branch = None
    for n in range(3):
        cut = slice(n * 512, (n + 1) * 512)
        h = matmul(normed1, w1v[:, cut])
        h = (0.5 * h * (1.0 + lax.erf(h * 0.7071067811865476))).astype(bf16)
        part = matmul(h, w2v[cut, :])
        branch = part if branch is None else branch + part
    masked = ext[3:6].reshape(TOK, C)
    section = (masked + scv[...][None, :] * branch).astype(bf16)
    sec[...] = section
    normed2 = layer_norm(section.astype(f32)).astype(bf16)
    n2buf[1] = normed2

    flags = tis[...].astype(f32)
    before = lax.broadcasted_iota(jnp.int32, (GW, GW), 0) < lax.broadcasted_iota(jnp.int32, (GW, GW), 1)
    rank = matmul(flags.astype(bf16), jnp.where(before, 1.0, 0.0).astype(bf16))
    counts = jnp.sum(flags, axis=1, keepdims=True)
    slot = lax.broadcasted_iota(jnp.int32, (CAP, GW), 0).astype(f32)
    x = jnp.zeros((CAP, C), f32)
    offset = jnp.zeros((1, 1), f32)
    for r in range(ROWS):
        pick = (slot == rank[r : r + 1, :] + offset) & (flags[r : r + 1, :] > 0)
        x = x + matmul(jnp.where(pick, 1.0, 0.0).astype(bf16), normed2[r * GW : (r + 1) * GW, :])
        offset = offset + counts[r : r + 1, :]
    empty = (lax.broadcasted_iota(jnp.int32, (CAP, C), 0).astype(f32) >= offset) & (
        lax.broadcasted_iota(jnp.int32, (CAP, C), 1) == 0)
    x = jnp.where(empty, MARK, x).astype(bf16)

    own = xbuf.at[0, pl.ds(pl.multiple_of(core * CAP, CAP), CAP)]
    far = xbuf.at[0, pl.ds(pl.multiple_of(UNIT + core * CAP, CAP), CAP)]
    xbuf[0, pl.ds(pl.multiple_of(core * CAP, CAP), CAP), :] = x
    own_copy = misc(own, own, 4, partner)
    far_copy = misc(own, far, 5, yoth)
    far_share = misc(far, far, 6, partner)
    n2_copy = misc(n2buf.at[1], n2buf.at[0], 7, partner)
    att_copy = misc(att_out, att_in, 8, partner)

    def block(c, way):
        return xbuf.at[c, pl.ds(pl.multiple_of(way * UNIT + core * CAP, CAP), CAP)]

    def hop(src, way, dst):
        at = way * NCHUNK + dst
        return remote(src, block(dst, way), ring_s.at[at], ring_r.at[at], along[way])

    def ring(way, src, dst):
        return hop(block(src, way), way, dst)

    def share(way, c):
        at = way * NCHUNK + c
        return remote(block(c, way), block(c, way), par_s.at[at], par_r.at[at], partner)

    for way in range(2):
        hop(own, way, 1).start()
    far_copy.start()
    own_copy.start()
    n2_copy.start()

    loads[6].wait()
    lane = lax.broadcasted_iota(jnp.int32, (TOK, QW), 1)

    def queries(group, normed):
        cut = slice((group % 2) * QW, (group % 2 + 1) * QW)
        query = matmul(normed, wqv[:, cut]).astype(bf16).astype(f32) * 0.125
        for h in range(4):
            inside = (lane >= h * HD) & (lane < (h + 1) * HD)
            qblk[group, h * TOK : (h + 1) * TOK, :] = jnp.where(inside, query, 0.0).astype(bf16)

    for group in (2, 3):
        queries(group, normed2)
    m_ref[...] = jnp.full(m_ref.shape, NEG, f32)
    l_ref[...] = jnp.zeros(l_ref.shape, f32)
    acc[...] = jnp.zeros(acc.shape, f32)

    n2_copy.wait_recv()
    for group in (0, 1):
        queries(group, n2buf[0])
    for way in range(2):
        ring(way, 1, 1).wait_recv()
        ring(way, 1, 3).start()
        share(way, 1).start()
    far_copy.wait_recv()
    far_share.start()
    for way in range(2):
        hop(far, way, 2).start()
    loads[7].wait()
    loads[8].wait()

    first_lane = jnp.where(lax.broadcasted_iota(jnp.int32, (8, C), 1) == 0, 1.0, 0.0).astype(bf16)

    def project(p):
        rows = pl.ds(pl.multiple_of(p * KS, KS), KS)
        xc = xbuf[pl.ds(2 * p, 2)].reshape(KS, C)
        for n in range(2):
            cut = slice(n * 256, (n + 1) * 256)
            k_all[rows, cut] = matmul(xc, wkv[:, cut]).astype(bf16)
            v_all[rows, cut] = matmul(xc, wvv[:, cut]).astype(bf16)

    own_copy.wait_recv()
    for way in range(2):
        share(way, 1).wait_recv()
    far_share.wait_recv()
    project(0)

    half_lane = lax.broadcasted_iota(jnp.int32, (TOK, 128), 1) < HD

    def score_part(p, g, n):
        rows = pl.ds(pl.multiple_of(p * KS + n * 256, 256), 256)
        s_ref[g % 2, :, n * 256 : (n + 1) * 256] = lax.dot_general(
            qblk[g], k_all[rows, (g % 2) * QW : (g % 2 + 1) * QW], LAST, preferred_element_type=f32)

    def scores(p, g):
        for n in range(3):
            score_part(p, g, n)

    def weigh(p, g):
        at = g % 2
        rows = pl.ds(pl.multiple_of(p * KS, KS), KS)
        o = matmul(p_ref[at], v_all[rows, (g % 2) * QW : (g % 2 + 1) * QW])
        for t in range(2):
            a, b = slice(2 * t * TOK, (2 * t + 1) * TOK), slice((2 * t + 1) * TOK, (2 * t + 2) * TOK)
            cut = slice(t * 128, (t + 1) * 128)
            o_t = jnp.where(half_lane, o[a, cut], o[b, cut])
            f_t = jnp.where(half_lane, a_ref[at, a, :], a_ref[at, b, :])
            dst = slice((g % 2) * QW + t * 128, (g % 2) * QW + (t + 1) * 128)
            acc[g // 2, :, dst] = acc[g // 2, :, dst] * f_t + o_t

    def attend(p, g, shift, ahead=None, behind=None):
        at = g % 2
        tiles = range(KS // 128)
        for r in range(0, 4 * TOK, 32):
            rs = slice(r, r + 32)
            if ahead is not None and r % 256 == 0:
                score_part(*ahead, r // 256)
            if behind is not None and r == 128:
                weigh(*behind)
            st = [
                (s_ref[at, rs, t * 128 : (t + 1) * 128].reshape(4, 8, 128)
                 + shift[:, t * 128 : (t + 1) * 128][None]).reshape(32, 128)
                for t in tiles
            ]
            top = functools.reduce(jnp.maximum, st)
            old = m_ref[g, rs, :]
            new = jnp.maximum(old, jnp.max(top, axis=1, keepdims=True))
            factor = jnp.exp(old - new)
            m_ref[g, rs, :] = new
            a_ref[at, rs, :] = factor
            total = None
            for t in tiles:
                weight = jnp.exp(st[t] - new)
                p_ref[at, rs, t * 128 : (t + 1) * 128] = weight.astype(bf16)
                total = weight if total is None else total + weight
            l_ref[g, rs, :] = l_ref[g, rs, :] * factor + total
    def mask(p):
        marks = [
            lax.dot_general(first_lane, xbuf[2 * p + i], LAST, preferred_element_type=f32) for i in range(2)
        ]
        return jnp.where(jnp.concatenate(marks, axis=1) > 0.5 * MARK, NEG, 0.0)

    scores(0, 0)

    @pl.loop(0, 3)
    def _(p):
        even, odd = 2 * p + 2, 2 * p + 3
        shift = mask(p)

        def take(c):
            for way in range(2):
                ring(way, c, c).wait_recv()

            @pl.when(c < 6)
            def _():
                ring(0, c, c + 2).start()

            ring(1, c, lax.min(c + 2, 7)).start()
            for way in range(2):
                share(way, c).start()

        attend(p, 0, shift, (p, 1))

        @pl.when(p == 0)
        def _():
            take(even)

        attend(p, 1, shift, (p, 2), (p, 0))
        for way in range(2):
            ring(way, odd, odd).wait_recv()

        @pl.when(p < 2)
        def _():
            ring(0, odd, odd + 2).start()

        @pl.when(p == 0)
        def _():
            ring(1, odd, odd + 2).start()

        for way in range(2):
            share(way, odd).start()

        attend(p, 2, shift, (p, 3), (p, 1))
        for way in range(2):
            share(way, even).wait_recv()
            share(way, odd).wait_recv()
        project(p + 1)

        @pl.when(p < 2)
        def _():
            take(even + 2)

        attend(p, 3, shift, (p + 1, 0), (p, 2))
        weigh(p, 3)

    def attended(who):
        parts = []
        for g in (2 * who, 2 * who + 1):
            for t in range(2):
                a, b = slice(2 * t * TOK, (2 * t + 1) * TOK), slice((2 * t + 1) * TOK, (2 * t + 2) * TOK)
                total_a = jnp.sum(l_ref[g, a, :], axis=1, keepdims=True)
                total_b = jnp.sum(l_ref[g, b, :], axis=1, keepdims=True)
                dst = slice((g % 2) * QW + t * 128, (g % 2) * QW + (t + 1) * 128)
                parts.append((acc[who, :, dst] / jnp.where(half_lane, total_a, total_b)).astype(bf16))
        return jnp.concatenate(parts, axis=1)

    shift = mask(3)
    attend(3, 0, shift, (3, 1))
    attend(3, 1, shift, (3, 2), (3, 0))
    weigh(3, 1)
    att_out[...] = attended(0)
    att_copy.start()
    attend(3, 2, shift, (3, 3))
    attend(3, 3, shift, None, (3, 2))
    weigh(3, 3)

    loads[9].wait()
    loads[10].wait()
    result = sec[...].astype(f32) + matmul(attended(1), wov[0])
    att_copy.wait_recv()
    result = result + matmul(att_in[...], wov[1])
    out[...] = result.astype(bf16).reshape(ROWS, GW, C)

    for copy in halos + [own_copy, far_copy, far_share, n2_copy, att_copy]:
        copy.wait_send()
    for c in range(1, NCHUNK):
        for way in range(2):
            ring(way, c, c).wait_send()
            share(way, c).wait_send()


def local(tokens, tissue, dw_kernel, w_fc1, w_fc2, layer_scale, w_query, w_key, w_value, w_out):
    vmem, sem = pltpu.VMEM, pltpu.SemaphoreType.DMA
    return pl.pallas_call(
        kernel,
        out_shape=jax.ShapeDtypeStruct((ROWS, GW, C), bf16),
        in_specs=[pl.BlockSpec(memory_space=pl.ANY)] * 10,
        out_specs=pl.BlockSpec(memory_space=pltpu.VMEM),
        scratch_shapes=[
            vmem((ROWS, GW, C), bf16), vmem((ROWS, GW), jnp.int32),
            vmem((7, 7, C), bf16), vmem((7, 7, C), f32),
            vmem((C, HID), bf16), vmem((HID, C), bf16), vmem((C,), f32),
            vmem((C, HALF), bf16), vmem((C, HALF), bf16), vmem((C, HALF), bf16), vmem((2, HALF, C), bf16),
            vmem((2, ROWS, GW, C), bf16), vmem((2, ROWS, GW), jnp.int32),
            vmem((9, GW, C), f32), vmem((TOK, C), f32), vmem((TOK, C), bf16),
            vmem((2, TOK, C), bf16), vmem((NCHUNK, CHUNK, C), bf16),
            vmem((NCHUNK * CHUNK, HALF), bf16), vmem((NCHUNK * CHUNK, HALF), bf16),
            vmem((GROUPS, 4 * TOK, QW), bf16),
            vmem((2, 4 * TOK, KS), f32), vmem((2, 4 * TOK, KS), bf16),
            vmem((GROUPS, 4 * TOK, 128), f32), vmem((GROUPS, 4 * TOK, 128), f32),
            vmem((2, 4 * TOK, 128), f32), vmem((2, TOK, HALF), f32),
            vmem((TOK, HALF), bf16), vmem((TOK, HALF), bf16),
            sem((11,)), sem((9,)), sem((9,)), sem((2 * NCHUNK,)), sem((2 * NCHUNK,)), sem((2 * NCHUNK,)), sem((2 * NCHUNK,)),
        ],
        compiler_params=pltpu.CompilerParams(
            collective_id=0, has_side_effects=True, vmem_limit_bytes=60 << 20),
        name="block",
    )(tokens, tissue, dw_kernel, w_fc1, w_fc2, layer_scale, w_query, w_key, w_value, w_out)


def solution(mesh):
    spec = P(("slide", "tile"), None, None)
    in_specs = (spec, P(("slide", "tile"), None)) + (P(),) * 8
    return jax.shard_map(local, mesh=mesh, in_specs=in_specs, out_specs=spec, check_vma=False)
```
